32 devices in a mesh: seq: 4 (over x, core), fsdp: 8 (over z, y).
Axes of the slice: x: 2, y: 2, z: 4, core: 2. Of those that a mesh axis runs over, the one named last changes fastest.
Arguments:
- tokens: bfloat16 [3, 8, 1024, 1024], P(None, None, ('seq', 'fsdp')), may hold values from -6 to 6
- cotangent: bfloat16 [3, 8, 1024, 1024], P(None, 'fsdp', 'seq'), may hold values from -6 to 6
- seq_lengths: int32 [3, 8], replicated, may hold values from 256 to 1024, as said below
- seq_slots: int32 [3, 8], replicated, may hold values from 0 to 7, each once within a row
- norm_gain: bfloat16 [1024], P(('seq', 'fsdp')), may hold values from 0.5 to 1.5
- w_query: bfloat16 [1024, 1024], P(('seq', 'fsdp')), may hold values from -0.1875 to 0.1875
- w_key: bfloat16 [1024, 1024], P(('seq', 'fsdp')), may hold values from -0.1875 to 0.1875
- w_value: bfloat16 [1024, 2048], P(('seq', 'fsdp')), may hold values from -0.1875 to 0.1875
- w_decay: bfloat16 [1024, 8], P(('seq', 'fsdp')), may hold values from -0.1875 to 0.1875
- w_beta: bfloat16 [1024, 8], P(('seq', 'fsdp')), may hold values from -0.1875 to 0.1875
- w_outgate: bfloat16 [1024, 2048], P(('seq', 'fsdp')), may hold values from -0.1875 to 0.1875
- query_filter: bfloat16 [4, 1024], P(None, ('seq', 'fsdp')), may hold values from -2.5 to 2.5
- key_filter: bfloat16 [4, 1024], P(None, ('seq', 'fsdp')), may hold values from -2.5 to 2.5
- value_filter: bfloat16 [4, 2048], P(None, ('seq', 'fsdp')), may hold values from -2.5 to 2.5
- decay_log: float32 [8], replicated, may hold values from -5 to 0
- decay_bias: float32 [8], replicated, may hold values from -6 to 0
- head_gain: bfloat16 [256], replicated, may hold values from 0.5 to 1.5
- w_output: bfloat16 [2048, 1024], P(None, ('seq', 'fsdp')), may hold values from -0.1875 to 0.1875
- ffn_gain: bfloat16 [1024], P(('seq', 'fsdp')), may hold values from 0.5 to 1.5
- w_gate: bfloat16 [1024, 2816], P(('seq', 'fsdp')), may hold values from -0.1875 to 0.1875
- w_up: bfloat16 [1024, 2816], P(('seq', 'fsdp')), may hold values from -0.1875 to 0.1875
- w_down: bfloat16 [2816, 1024], P(None, ('seq', 'fsdp')), may hold values from -0.15625 to 0.15625
Outputs:
- mixed: float32 [3, 8, 1024, 1024], P(None, 'fsdp', 'seq')
- tokens_grad: float32 [3, 8, 1024, 1024], P(None, None, ('seq', 'fsdp'))
- norm_gain_grad: float32 [1024], P(('seq', 'fsdp'))
- query_grad: float32 [1024, 1024], P(('seq', 'fsdp'))
- key_grad: float32 [1024, 1024], P(('seq', 'fsdp'))
- value_grad: float32 [1024, 2048], P(('seq', 'fsdp'))
- decay_grad: float32 [1024, 8], P(('seq', 'fsdp'))
- beta_grad: float32 [1024, 8], P(('seq', 'fsdp'))
- outgate_grad: float32 [1024, 2048], P(('seq', 'fsdp'))
- query_filter_grad: float32 [4, 1024], P(None, ('seq', 'fsdp'))
- key_filter_grad: float32 [4, 1024], P(None, ('seq', 'fsdp'))
- value_filter_grad: float32 [4, 2048], P(None, ('seq', 'fsdp'))
- decay_log_grad: float32 [8], replicated
- decay_bias_grad: float32 [8], replicated
- head_gain_grad: float32 [256], replicated
- output_grad: float32 [2048, 1024], P(None, ('seq', 'fsdp'))
- ffn_gain_grad: float32 [1024], P(('seq', 'fsdp'))
- gate_grad: float32 [1024, 2816], P(('seq', 'fsdp'))
- up_grad: float32 [1024, 2816], P(('seq', 'fsdp'))
- down_grad: float32 [2816, 1024], P(None, ('seq', 'fsdp'))
The draws below stay inside these ranges and needn't reach their ends.
Inputs may be any that keep to these rules, and one draw needn't show every extreme that they name: `seq_lengths`: every length is at least 256; in each micro-batch some sequence has exactly 1024. `seq_slots`: each micro-batch's row is a permutation of the slots; slots j * 1 to (j + 1) - 1 form sequence group j.
All inputs are finite; a program needn't handle non-finite values.
Results may differ from the reference program's by a relative error of at most 0.02.
Values may be sent and summed in bfloat16 or wider, within the bound.
A program may use at most 256 MiB of HBM per device.

```python
import jax
import jax.numpy as jnp
from jax import lax

D = 1024
HEADS = 8
DK = 128
DV = 256
FF = 2816
CONV = 4
SPAN = 64
BLOCK = 1024
MICRO = 3
SEQ_GROUP = 1
SLOTS = 8
N_FSDP = 8


def draw_seq_lengths(key, part):
    draw_key, pick_key = jax.random.split(key)
    values = jax.random.randint(draw_key, (MICRO, SLOTS), BLOCK // 4, BLOCK + 1)
    longest = jax.random.randint(pick_key, (MICRO, 1), 0, SLOTS)
    places = jnp.arange(SLOTS, dtype=jnp.int32)[None, :]
    return jnp.where(places == longest, BLOCK, values).astype(jnp.int32)


def levels(rng, extent, cuts, least, top_value):
    level, own = 1.0, jax.random.fold_in(rng, 6)
    for axis_at, shards_of in cuts:
        steps = jnp.exp(jax.random.uniform(jax.random.fold_in(own, axis_at), (shards_of,), jnp.float32, least / len(cuts), top_value / len(cuts)))
        level = level * jnp.repeat(steps, extent[axis_at] // shards_of).reshape([-1 if axis == axis_at else 1 for axis in range(len(extent))])
    return level


def centred(stream_key, extent, scale, reach, cuts=(), kind=jnp.bfloat16):
    values = jax.random.normal(stream_key, extent, jnp.float32) * scale
    if len(cuts) > 0:
        values = levels(stream_key, extent, cuts, -0.22, 0.18) * values
    return jnp.clip(values, min=-reach, max=reach).astype(kind)


def setup_inputs(seed: int = 0) -> dict:
    key_list = jax.random.split(jax.random.key(seed), 23)
    tokens = centred(key_list[0], (MICRO, SLOTS, BLOCK, D), 1.0, 6.0, ((2, 32),))
    cotangent = centred(key_list[1], (MICRO, SLOTS, BLOCK, D), 1.0, 6.0, ((1, 8), (2, 4)))
    seq_lengths = draw_seq_lengths(jax.random.fold_in(key_list[22], 71), 0)
    seq_slots = jax.vmap(lambda own: jax.random.permutation(own, SLOTS))(jax.random.split(key_list[3], MICRO)).reshape((MICRO, SLOTS)).astype(jnp.int32)
    norm_gain = jnp.clip(1.0 + 0.1 * jax.random.normal(key_list[4], (D,), jnp.float32), 0.5, 1.5).astype(jnp.bfloat16)
    w_query = centred(key_list[5], (D, HEADS * DK), D ** -0.5, 0.1875, ((0, 32),))
    w_key = centred(key_list[6], (D, HEADS * DK), D ** -0.5, 0.1875, ((0, 32),))
    w_value = centred(key_list[7], (D, HEADS * DV), D ** -0.5, 0.1875, ((0, 32),))
    w_decay = centred(key_list[8], (D, HEADS), D ** -0.5, 0.1875, ((0, 32),))
    w_beta = centred(key_list[9], (D, HEADS), D ** -0.5, 0.1875, ((0, 32),))
    w_outgate = centred(key_list[10], (D, HEADS * DV), D ** -0.5, 0.1875, ((0, 32),))
    query_filter = centred(key_list[11], (CONV, HEADS * DK), 0.5, 2.5, ((1, 32),))
    key_filter = centred(key_list[12], (CONV, HEADS * DK), 0.5, 2.5, ((1, 32),))
    value_filter = centred(key_list[13], (CONV, HEADS * DV), 0.5, 2.5, ((1, 32),))
    decay_log = jnp.clip(jax.random.uniform(key_list[14], (HEADS,), jnp.float32, -5.0, 0.0), -5.0, 0.0)
    decay_bias = jnp.clip(jax.random.uniform(key_list[15], (HEADS,), jnp.float32, -6.0, 0.0), -6.0, 0.0)
    head_gain = jnp.clip(1.0 + 0.1 * jax.random.normal(key_list[16], (DV,), jnp.float32), 0.5, 1.5).astype(jnp.bfloat16)
    w_output = centred(key_list[17], (HEADS * DV, D), (HEADS * DV // 2) ** -0.5, 0.1875, ((1, 32),))
    ffn_gain = jnp.clip(1.0 + 0.1 * jax.random.normal(key_list[18], (D,), jnp.float32), 0.5, 1.5).astype(jnp.bfloat16)
    w_gate = centred(key_list[19], (D, FF), D ** -0.5, 0.1875, ((0, 32),))
    w_up = centred(key_list[20], (D, FF), D ** -0.5, 0.1875, ((0, 32),))
    w_down = centred(key_list[21], (FF, D), (FF // 2) ** -0.5, 0.15625, ((1, 32),))
    return dict(tokens=tokens, cotangent=cotangent, seq_lengths=seq_lengths, seq_slots=seq_slots, norm_gain=norm_gain, w_query=w_query, w_key=w_key, w_value=w_value, w_decay=w_decay, w_beta=w_beta, w_outgate=w_outgate, query_filter=query_filter, key_filter=key_filter, value_filter=value_filter, decay_log=decay_log, decay_bias=decay_bias, head_gain=head_gain, w_output=w_output, ffn_gain=ffn_gain, w_gate=w_gate, w_up=w_up, w_down=w_down)


EPS = 1e-06
HIGH = lax.Precision.HIGHEST

@jax.custom_vjp
def low(v):
    return lax.optimization_barrier(v.astype(jnp.bfloat16)).astype(jnp.float32)

@jax.custom_vjp
def low_back(v):
    return v

def low_keep(v):
    return (low(v), None)

def low_pass(kept, grad):
    return (grad,)

def back_keep(v):
    return (v, None)

def back_low(kept, grad):
    return (low(grad),)
low.defvjp(low_keep, low_pass)
low_back.defvjp(back_keep, back_low)

def rms_scale(values, gain):
    return values * lax.rsqrt(lax.optimization_barrier(jnp.mean(values * values, -1, keepdims=True)) + EPS) * gain

def gated_norm(values, gate_pre, gain):
    head_size = gain.shape[0]
    split_vals = values.reshape(values.shape[:-1] + (values.shape[-1] // head_size, head_size))
    scaled = split_vals * lax.rsqrt(lax.optimization_barrier(jnp.mean(split_vals * split_vals, -1, keepdims=True)) + EPS) * gain
    return scaled.reshape(values.shape) * jax.nn.silu(gate_pre)

def swish_gate(gate_val, upper_val):
    return jax.nn.silu(gate_val) * upper_val

def causal_filter(series, taps_weight):
    tap_count = taps_weight.shape[0]
    seq_len = series.shape[1]
    padded = jnp.pad(series, ((0, 0), (tap_count - 1, 0), (0, 0)))
    running = padded[:, 0:seq_len, :] * taps_weight[0]
    for offset in range(1, tap_count):
        running = running + padded[:, offset:offset + seq_len, :] * taps_weight[offset]
    return jax.nn.silu(running)

def span_step(memory, pieces):
    query_in, keys_in, values_in, log_decay, beta_rate = pieces
    span_len = log_decay.shape[-1]
    log_cumul = jnp.cumsum(log_decay, -1)
    row_ids = jnp.arange(span_len)[:, None]
    col_ids = jnp.arange(span_len)[None, :]
    lower_mask = row_ids >= col_ids
    strict_mask = row_ids > col_ids
    log_gap = log_cumul[..., :, None] - log_cumul[..., None, :]
    decay = jnp.where(lower_mask, jnp.exp(jnp.where(lower_mask, log_gap, 0.0)), 0.0)
    keys_dot = jnp.einsum('bhid,bhjd->bhij', keys_in, keys_in, precision=HIGH)
    mixing = jnp.eye(span_len, dtype=jnp.float32) + beta_rate[..., :, None] * jnp.where(strict_mask, decay * keys_dot, 0.0)
    growth = jnp.exp(log_cumul)
    target = beta_rate[..., None] * (values_in - growth[..., None] * jnp.einsum('bhid,bhde->bhie', keys_in, memory, precision=HIGH))
    update = lax.linalg.triangular_solve(mixing, target, left_side=True, lower=True, unit_diagonal=True)
    scores = jnp.where(lower_mask, decay * jnp.einsum('bhid,bhjd->bhij', query_in, keys_in, precision=HIGH), 0.0)
    output = growth[..., None] * jnp.einsum('bhid,bhde->bhie', query_in, memory, precision=HIGH)
    output = output + jnp.einsum('bhij,bhje->bhie', scores, update, precision=HIGH)
    last_log = log_cumul[..., -1:]
    carried = keys_in * jnp.exp(last_log - log_cumul)[..., None]
    memory = jnp.exp(last_log)[..., None] * memory + jnp.einsum('bhid,bhie->bhde', carried, update, precision=HIGH)
    return (memory, output)

def delta_rule(query_in, keys_in, values_in, log_decay, beta_rate):
    batch, seq_len, heads, key_dim = query_in.shape
    value_dim = values_in.shape[-1]
    count = seq_len // SPAN

    def blocks_four(array):
        return array.reshape((batch, count, SPAN, heads, array.shape[-1])).transpose(1, 0, 3, 2, 4)

    def blocks_three(array):
        return array.reshape((batch, count, SPAN, heads)).transpose(1, 0, 3, 2)
    start = jnp.zeros((batch, heads, key_dim, value_dim), jnp.float32)
    _, outputs = lax.scan(jax.checkpoint(span_step), start, (blocks_four(query_in), blocks_four(keys_in), blocks_four(values_in), blocks_three(log_decay), blocks_three(beta_rate)))
    return outputs.transpose(1, 0, 3, 2, 4).reshape(batch, seq_len, heads * value_dim)

def mixer(query_pre, key_pre, value_pre, decay_pre, beta_pre, filter_query, filter_key, filter_value, decay_log, decay_bias):
    batch, seq_len, _ = query_pre.shape
    heads = decay_pre.shape[-1]
    query_conv = causal_filter(query_pre, filter_query).reshape(batch, seq_len, heads, -1)
    key_conv = causal_filter(key_pre, filter_key).reshape(batch, seq_len, heads, -1)
    value_conv = causal_filter(value_pre, filter_value).reshape(batch, seq_len, heads, -1)
    query_hat = query_conv * lax.rsqrt(lax.optimization_barrier(jnp.sum(query_conv * query_conv, -1, keepdims=True)) + EPS) * query_conv.shape[-1] ** (-0.5)
    key_hat = key_conv * lax.rsqrt(lax.optimization_barrier(jnp.sum(key_conv * key_conv, -1, keepdims=True)) + EPS)
    beta_rate = jax.nn.sigmoid(beta_pre)
    log_decay = -jnp.exp(decay_log) * jax.nn.softplus(decay_pre + decay_bias)
    return delta_rule(query_hat, key_hat, value_conv, log_decay, beta_rate)

def project(left, right):
    return jnp.einsum('bld,dc->blc', left, right, precision=HIGH)

def forward(params, inputs):
    norm_gain, w_query, w_key, w_value, w_decay, w_beta, w_outgate, query_filter, key_filter, value_filter, decay_log, decay_bias, head_gain, w_output, ffn_gain, w_gate, w_up, w_down = params
    normed = low(rms_scale(inputs, norm_gain))
    query_pre = low_back(low(project(normed, w_query)))
    key_pre = low_back(low(project(normed, w_key)))
    value_pre = low_back(low(project(normed, w_value)))
    decay_pre = low_back(low(project(normed, w_decay)))
    beta_pre = low_back(low(project(normed, w_beta)))
    outgate_pre = low_back(project(normed, w_outgate))
    mixed_heads = mixer(query_pre, key_pre, value_pre, decay_pre, beta_pre, query_filter, key_filter, value_filter, decay_log, decay_bias)
    mixed_heads = low_back(low(mixed_heads))
    gated_rows = low(gated_norm(mixed_heads, outgate_pre, head_gain))
    attended = inputs + low_back(project(gated_rows, w_output))
    ffn_in = low(rms_scale(attended, ffn_gain))
    gate_val = low_back(project(ffn_in, w_gate))
    upper_val = low_back(project(ffn_in, w_up))
    hidden = low(swish_gate(gate_val, upper_val))
    return attended + low_back(project(hidden, w_down))

def take_rows(source, order):
    return jnp.take(source, order, axis=0)

def reference(tokens, cotangent, seq_lengths, seq_slots, norm_gain, w_query, w_key, w_value, w_decay, w_beta, w_outgate, query_filter, key_filter, value_filter, decay_log, decay_bias, head_gain, w_output, ffn_gain, w_gate, w_up, w_down):
    params = (norm_gain.astype(jnp.float32), w_query.astype(jnp.float32), w_key.astype(jnp.float32), w_value.astype(jnp.float32), w_decay.astype(jnp.float32), w_beta.astype(jnp.float32), w_outgate.astype(jnp.float32), query_filter.astype(jnp.float32), key_filter.astype(jnp.float32), value_filter.astype(jnp.float32), decay_log.astype(jnp.float32), decay_bias.astype(jnp.float32), head_gain.astype(jnp.float32), w_output.astype(jnp.float32), ffn_gain.astype(jnp.float32), w_gate.astype(jnp.float32), w_up.astype(jnp.float32), w_down.astype(jnp.float32))
    slot_ids = jnp.arange(SLOTS, dtype=jnp.int32)
    matches = seq_slots[:, :, None] == slot_ids[None, None, :]
    source_of = lax.optimization_barrier(jnp.sum(jnp.where(matches, slot_ids[None, :, None], 0), axis=1)).astype(jnp.int32)
    slot_length = lax.optimization_barrier(jnp.sum(jnp.where(matches, seq_lengths[:, :, None], 0), axis=1)).astype(jnp.int32)
    grouped = jax.vmap(take_rows)(tokens, source_of)
    row_ids = jnp.arange(BLOCK, dtype=jnp.int32)
    valid_rows = (row_ids[None, None, :] < slot_length[:, :, None]).astype(jnp.float32)[..., None]
    group_total = MICRO * N_FSDP
    inputs_all = grouped.reshape(group_total, SEQ_GROUP, BLOCK, D)
    cot_all = (cotangent.astype(jnp.float32) * valid_rows).reshape(group_total, SEQ_GROUP, BLOCK, D)

    def group_pass(running, item_pair):
        inputs, cot_rows = item_pair
        output, pullback = jax.vjp(forward, params, inputs.astype(jnp.float32))
        grad_params, grad_inputs = pullback(cot_rows)
        return (jax.tree.map(jnp.add, running, grad_params), (output, grad_inputs))
    zeros = jax.tree.map(jnp.zeros_like, params)
    grads, (outputs, input_grads) = lax.scan(group_pass, zeros, (inputs_all, cot_all))
    mixed = outputs.reshape(MICRO, SLOTS, BLOCK, D) * valid_rows
    slot_grad = input_grads.reshape(MICRO, SLOTS, BLOCK, D)
    tokens_grad = jax.vmap(take_rows)(slot_grad, seq_slots)
    return (mixed, tokens_grad, grads[0], grads[1], grads[2], grads[3], grads[4], grads[5], grads[6], grads[7], grads[8], grads[9], grads[10], grads[11], grads[12], grads[13], grads[14], grads[15], grads[16], grads[17])
```

```python
import functools
import jax
import jax.numpy as jnp
from jax import lax
from jax.experimental import pallas as pl
from jax.experimental.pallas import tpu as pltpu
from jax.sharding import PartitionSpec as P

EPS = 1e-6
C = 128
KD = 128
VD = 256
F32 = jnp.float32
BF = jnp.bfloat16
HIGHEST = lax.Precision.HIGHEST

def iota(shape, dim):
    return lax.broadcasted_iota(jnp.int32, shape, dim)

def mm(a, b, ca=1, cb=0):
    return lax.dot_general(a.astype(BF), b.astype(BF), (((ca,), (cb,)), ((), ())), preferred_element_type=F32)

def exact(a, b):
    return lax.dot_general(a, b, (((1,), (0,)), ((), ())), precision=HIGHEST, preferred_element_type=F32)

def unit_inverse(low):
    rows, cols = iota((C, C), 0), iota((C, C), 1)
    diag = jnp.where(rows // 16 == cols // 16, low, 0.0)
    packed = jnp.sum(diag.reshape(C // 16, 16, C), axis=0)
    prow, pcol = iota((16, C), 0), iota((16, C), 1)
    inv = jnp.where(prow == pcol % 16, 1.0, 0.0).astype(F32)
    base = (pcol // 16) * 16
    for j in range(15):
        col = jnp.take_along_axis(packed, base + j, axis=1)
        inv = inv - col * inv[j:j + 1, :]
    full = jnp.broadcast_to(inv[None], (C // 16, 16, C)).reshape(C, C)
    full = jnp.where(rows // 16 == cols // 16, full, 0.0)
    size = 16
    while size < C:
        off = jnp.where((rows // (2 * size) == cols // (2 * size)) & (rows // size == cols // size + 1), low, 0.0)
        full = full - mm(mm(full, off), full)
        size *= 2
    return full

def gates(pre, dlog, dbias):
    arg = pre + dbias
    soft = jnp.maximum(arg, 0.0) + jnp.log1p(jnp.exp(-jnp.abs(arg)))
    log_decay = -jnp.exp(dlog) * soft
    rows, cols = iota((C, C), 0), iota((C, C), 1)
    tri = jnp.where(rows >= cols, 1.0, 0.0).astype(F32)
    cum = exact(tri, log_decay)
    return log_decay, cum

def sig(x):
    return 1.0 / (1.0 + jnp.exp(-x))

def conv_taps(ext_ref, taps, width):
    acc = ext_ref[pl.ds(5, C), :] * taps[0:1, :]
    for i in range(1, 4):
        acc = acc + ext_ref[pl.ds(5 + i, C), :] * taps[i:i + 1, :]
    return acc

def load_ext(qkv, halo, ext_ref, first):
    ahead = halo[8:16, :].astype(F32)
    ext_ref[pl.ds(0, 8), :] = jnp.where(first, 0.0, ahead)
    ext_ref[pl.ds(8, C), :] = qkv.astype(F32)

def forward_kernel(heads, micro, qkv_ref, halo_ref, og_ref, db_ref, taps_ref, small_ref, gain_ref,
                   gated_ref, mix_ref, inv_ref, upd_ref, state_ref, mem_ref, ext_ref):
    step = pl.program_id(0)
    first = step == 0

    @pl.when(first)
    def _():
        mem_ref[...] = jnp.zeros_like(mem_ref)

    taps = taps_ref[...]
    rows, cols = iota((C, C), 0), iota((C, C), 1)
    lower = rows >= cols
    gain = gain_ref[0:1, :]
    for m in range(micro):
        ext = ext_ref.at[m]
        load_ext(qkv_ref[m], halo_ref[m], ext, first)
        act = conv_taps(ext, taps, None)
        act = act * sig(act)
        pre = db_ref[m].astype(F32)
        _, cum = gates(pre, small_ref[0:1, :], small_ref[1:2, :])
        rate = sig(pre)
        cum_t = jnp.transpose(cum)
        for h in range(heads):
            u = m * heads + h
            q = act[:, h * KD:(h + 1) * KD]
            k = act[:, (heads + h) * KD:(heads + h + 1) * KD]
            v = act[:, 2 * heads * KD + h * VD:2 * heads * KD + (h + 1) * VD]
            q = q * (lax.rsqrt(jnp.sum(q * q, -1, keepdims=True) + EPS) * KD ** -0.5)
            k = k * lax.rsqrt(jnp.sum(k * k, -1, keepdims=True) + EPS)
            beta = rate[:, heads + h:heads + h + 1]
            gcol = cum[:, h:h + 1]
            grow = cum_t[h:h + 1, :]
            decay = jnp.where(lower, jnp.exp(jnp.where(lower, gcol - grow, 0.0)), 0.0)
            grow_col = jnp.exp(gcol)
            glast = cum[C - 1:C, h:h + 1]
            dots = mm(jnp.concatenate([k, q], 0), k, 1, 1)
            low = jnp.where(rows > cols, beta * decay * dots[:C], 0.0)
            scores = decay * dots[C:]
            inv = unit_inverse(low)
            mem = mem_ref[u]
            state_ref[0, u] = mem.astype(state_ref.dtype)
            from_mem = mm(jnp.concatenate([grow_col * k, grow_col * q], 0), mem)
            upd = mm(inv, beta * (v - from_mem[:C]))
            out = from_mem[C:] + mm(scores, upd)
            mem_ref[u] = jnp.exp(glast) * mem + mm(k * jnp.exp(glast - gcol), upd, 0, 0)
            inv_ref[0, u] = inv.astype(inv_ref.dtype)
            upd_ref[0, u] = upd.astype(upd_ref.dtype)
            mix = out.astype(BF)
            mix_ref[0, u] = mix
            mix = mix.astype(F32)
            og = og_ref[m, :, h * VD:(h + 1) * VD].astype(F32)
            scale = lax.rsqrt(jnp.mean(mix * mix, -1, keepdims=True) + EPS)
            gated = mix * scale * gain * (og * sig(og))
            gated_ref[0, m, :, h * VD:(h + 1) * VD] = gated.astype(BF)


def mixer_forward(pre, taps, small, gain, heads, shards):
    micro, length, _ = pre.shape
    count = length // C
    units = micro * heads
    qkv_cols, v_cols = heads * (2 * KD + VD), heads * VD
    per = count // shards
    lead = (2 * heads * KD + 2 * v_cols) // 128
    return pl.pallas_call(
        functools.partial(forward_kernel, heads, micro),
        grid=(count,),
        in_specs=[
            pl.BlockSpec((micro, C, qkv_cols), lambda c: (0, c, 0)),
            pl.BlockSpec((micro, 16, qkv_cols), lambda c: (0, jnp.maximum(c * (C // 16) - 1, 0), 0)),
            pl.BlockSpec((micro, C, v_cols), lambda c: (0, c, 2)),
            pl.BlockSpec((micro, C, 128), lambda c: (0, c, lead + 0)),
            pl.BlockSpec((8, qkv_cols), lambda c: (0, 0)),
            pl.BlockSpec((8, 128), lambda c: (0, 0)),
            pl.BlockSpec((8, VD), lambda c: (0, 0)),
        ],
        out_specs=[
            pl.BlockSpec((1, micro, C, v_cols), lambda c: (c // per, 0, c % per, 0)),
            pl.BlockSpec((1, units, C, VD), lambda c: (c, 0, 0, 0)),
            pl.BlockSpec((1, units, C, C), lambda c: (c, 0, 0, 0)),
            pl.BlockSpec((1, units, C, VD), lambda c: (c, 0, 0, 0)),
            pl.BlockSpec((1, units, KD, VD), lambda c: (c, 0, 0, 0)),
        ],
        out_shape=[
            jax.ShapeDtypeStruct((shards, micro, length // shards, v_cols), BF),
            jax.ShapeDtypeStruct((count, units, C, VD), BF),
            jax.ShapeDtypeStruct((count, units, C, C), BF),
            jax.ShapeDtypeStruct((count, units, C, VD), BF),
            jax.ShapeDtypeStruct((count, units, KD, VD), BF),
        ],
        scratch_shapes=[
            pltpu.VMEM((units, KD, VD), F32),
            pltpu.VMEM((micro, C + 8, qkv_cols), F32),
        ],
        compiler_params=pltpu.CompilerParams(
            dimension_semantics=("arbitrary",), vmem_limit_bytes=50 * 1024 * 1024
        ),
    )(pre, pre, pre, pre, taps, small, gain)


def backward_kernel(heads, micro, qkv_ref, halo_ref, og_ref, db_ref, dgated_ref, mix_ref, inv_ref, upd_ref, state_ref,
                    taps_ref, small_ref, gain_ref,
                    dpre_ref, dtaps_ref, dsmall_ref, dgain_ref, dmem_ref, ext_ref, dy_ref):
    step = pl.program_id(0)
    count = pl.num_programs(0)

    @pl.when(step == 0)
    def _():
        dmem_ref[...] = jnp.zeros_like(dmem_ref)
        dtaps_ref[...] = jnp.zeros_like(dtaps_ref)
        dsmall_ref[...] = jnp.zeros_like(dsmall_ref)
        dgain_ref[...] = jnp.zeros_like(dgain_ref)

    taps = taps_ref[...]
    rows, cols = iota((C, C), 0), iota((C, C), 1)
    lower = rows >= cols
    upper = jnp.where(rows <= cols, 1.0, 0.0).astype(F32)
    gain = gain_ref[0:1, :]
    qk_cols = heads * KD
    for m in range(micro):
        ext, dy = ext_ref.at[m], dy_ref.at[m]
        load_ext(qkv_ref[m], halo_ref[m], ext, step == count - 1)
        dy[pl.ds(C, 8), :] = jnp.where(step == 0, 0.0, dy[pl.ds(0, 8), :])
        conv = conv_taps(ext, taps, None)
        gate = sig(conv)
        act = conv * gate
        dgate = gate * (1.0 + conv * (1.0 - gate))
        pre = db_ref[m].astype(F32)
        log_decay, cum = gates(pre, small_ref[0:1, :], small_ref[1:2, :])
        rate = sig(pre)
        cum_t = jnp.transpose(cum)
        dcum = jnp.zeros((C, 128), F32)
        drate = jnp.zeros((C, 128), F32)
        for h in range(heads):
            u = m * heads + h
            q0 = act[:, h * KD:(h + 1) * KD]
            k0 = act[:, qk_cols + h * KD:qk_cols + (h + 1) * KD]
            v = act[:, 2 * qk_cols + h * VD:2 * qk_cols + (h + 1) * VD]
            qr = lax.rsqrt(jnp.sum(q0 * q0, -1, keepdims=True) + EPS)
            kr = lax.rsqrt(jnp.sum(k0 * k0, -1, keepdims=True) + EPS)
            qn, k = q0 * qr, k0 * kr
            q = qn * KD ** -0.5
            beta = rate[:, heads + h:heads + h + 1]
            gcol = cum[:, h:h + 1]
            grow = cum_t[h:h + 1, :]
            decay = jnp.where(lower, jnp.exp(jnp.where(lower, gcol - grow, 0.0)), 0.0)
            growth = jnp.exp(gcol)
            glast = cum[C - 1:C, h:h + 1]
            tail = jnp.exp(glast - gcol)
            dots = mm(jnp.concatenate([k, q], 0), k, 1, 1)
            near = jnp.where(rows > cols, decay * dots[:C], 0.0)
            scores = decay * dots[C:]
            mix = mix_ref[0, u].astype(F32)
            og = og_ref[m, :, h * VD:(h + 1) * VD].astype(F32)
            dgated = dgated_ref[0, m, :, h * VD:(h + 1) * VD].astype(F32)
            scale = lax.rsqrt(jnp.mean(mix * mix, -1, keepdims=True) + EPS)
            mixn = mix * scale
            osig = sig(og)
            dog = dgated * mixn * gain * (osig * (1.0 + og * (1.0 - osig)))
            dn = dgated * (og * osig)
            dgain_ref[0:1, :] += jnp.sum(dn * mixn, 0, keepdims=True)
            dn = dn * gain
            dout = scale * (dn - mixn * jnp.mean(dn * mixn, -1, keepdims=True))
            dout = dout.astype(BF)
            upd, mem, inv, dmem = upd_ref[0, u], state_ref[0, u], inv_ref[0, u], dmem_ref[u]
            dmem_low = dmem.astype(BF)
            both = jnp.concatenate([upd, mem], 0)
            one = mm(dout, both, 1, 1)
            dscores = jnp.where(lower, one[:, :C], 0.0)
            dq_in = one[:, C:]
            ktail = k * tail
            dupd = mm(scores, dout, 0, 0) + mm(ktail, dmem_low)
            dres = mm(inv, dupd, 0, 0)
            two = mm(dres, both, 1, 1)
            dlow = jnp.where(rows > cols, -two[:, :C], 0.0)
            dk_in = two[:, C:]
            kin, qin = growth * k, growth * q
            dk_scaled = -beta * dk_in
            dmem_new = jnp.exp(glast) * dmem + mm(qin, dout, 0, 0) - mm(beta * kin, dres, 0, 0)
            dk_tail = mm(upd, dmem_low, 1, 1)
            pull = dscores * scores
            pull_low = dlow * near
            pulls = pull + beta * pull_low
            in_parts = jnp.sum(dq_in * qin + dk_scaled * kin - dk_tail * ktail + pulls, -1, keepdims=True)
            tail_sum = jnp.sum(jnp.sum(dk_tail * ktail, -1, keepdims=True), 0, keepdims=True)
            mem_sum = jnp.sum(jnp.sum(dmem * mem.astype(F32), -1, keepdims=True), 0, keepdims=True)
            dcum_col = in_parts - jnp.transpose(jnp.broadcast_to(jnp.sum(pulls, 0, keepdims=True), (C, C)))[:, 0:1]
            last = iota((C, 1), 0) == C - 1
            dcum_col = dcum_col + jnp.where(last, tail_sum + jnp.exp(glast) * mem_sum, 0.0)
            dbeta = jnp.sum(dres * v, -1, keepdims=True) + jnp.sum(pull_low - dk_in * kin, -1, keepdims=True)
            lane = iota((C, 128), 1)
            dcum = jnp.where(lane == h, dcum_col, dcum)
            drate = jnp.where(lane == heads + h, dbeta, drate)
            dqk = dscores * decay
            dkk = dlow * decay * beta
            left = mm(jnp.concatenate([dqk, dkk], 0), k)
            dq = left[:C] + growth * dq_in
            dk = left[C:] + mm(dqk, q, 0, 0) + mm(dkk, k, 0, 0) + growth * dk_scaled + tail * dk_tail
            dv = beta * dres
            dmem_ref[u] = dmem_new
            dq = dq * KD ** -0.5
            dq = qr * (dq - qn * jnp.sum(dq * qn, -1, keepdims=True))
            dk = kr * (dk - k * jnp.sum(dk * k, -1, keepdims=True))
            for part, at, wide in ((dq, h * KD, KD), (dk, qk_cols + h * KD, KD), (dv, 2 * qk_cols + h * VD, VD)):
                dy[pl.ds(0, C), at:at + wide] = part * dgate[:, at:at + wide]
            at = 2 * qk_cols + heads * VD + h * VD
            dpre_ref[m, :, at:at + VD] = dog.astype(BF)
        grad = dy[pl.ds(0, C), :]
        dx = dy[pl.ds(3, C), :] * taps[0:1, :]
        for i in range(1, 4):
            dx = dx + dy[pl.ds(3 - i, C), :] * taps[i:i + 1, :]
        dpre_ref[m, :, 0:2 * qk_cols + heads * VD] = dx.astype(BF)
        for i in range(4):
            dtaps_ref[i:i + 1, :] += jnp.sum(grad * ext[pl.ds(5 + i, C), :], 0, keepdims=True)
        dlog = exact(upper, dcum)
        speed = -jnp.exp(small_ref[0:1, :])
        ddecay = dlog * speed * sig(pre + small_ref[1:2, :])
        dsmall_ref[0:1, :] += jnp.sum(dlog * log_decay, 0, keepdims=True)
        dsmall_ref[1:2, :] += jnp.sum(ddecay, 0, keepdims=True)
        ddb = ddecay + drate * rate * (1.0 - rate)
        at = 2 * qk_cols + 2 * heads * VD
        dpre_ref[m, :, at:at + 128] = ddb.astype(BF)


def mixer_backward(pre, dgated, saved, taps, small, gain, heads):
    mix, inv, upd, state = saved
    shards, micro, part, v_cols = dgated.shape
    length, width = pre.shape[1:]
    count = length // C
    units = micro * heads
    qkv_cols = heads * (2 * KD + VD)
    per = count // shards
    lead = (2 * heads * KD + 2 * v_cols) // 128
    end = count - 1
    keep = lambda *s: pl.BlockSpec((1, units) + s, lambda c: (end - c, 0, 0, 0))
    return pl.pallas_call(
        functools.partial(backward_kernel, heads, micro),
        grid=(count,),
        in_specs=[
            pl.BlockSpec((micro, C, qkv_cols), lambda c: (0, end - c, 0)),
            pl.BlockSpec((micro, 16, qkv_cols), lambda c: (0, jnp.maximum((end - c) * (C // 16) - 1, 0), 0)),
            pl.BlockSpec((micro, C, v_cols), lambda c: (0, end - c, 2)),
            pl.BlockSpec((micro, C, 128), lambda c: (0, end - c, lead)),
            pl.BlockSpec((1, micro, C, v_cols), lambda c: ((end - c) // per, 0, (end - c) % per, 0)),
            keep(C, VD), keep(C, C), keep(C, VD), keep(KD, VD),
            pl.BlockSpec((8, qkv_cols), lambda c: (0, 0)),
            pl.BlockSpec((8, 128), lambda c: (0, 0)),
            pl.BlockSpec((8, VD), lambda c: (0, 0)),
        ],
        out_specs=[
            pl.BlockSpec((micro, C, width), lambda c: (0, end - c, 0)),
            pl.BlockSpec((8, qkv_cols), lambda c: (0, 0)),
            pl.BlockSpec((8, 128), lambda c: (0, 0)),
            pl.BlockSpec((8, VD), lambda c: (0, 0)),
        ],
        out_shape=[
            jax.ShapeDtypeStruct((micro, length, width), BF),
            jax.ShapeDtypeStruct((8, qkv_cols), F32),
            jax.ShapeDtypeStruct((8, 128), F32),
            jax.ShapeDtypeStruct((8, VD), F32),
        ],
        scratch_shapes=[
            pltpu.VMEM((units, KD, VD), F32),
            pltpu.VMEM((micro, C + 8, qkv_cols), F32),
            pltpu.VMEM((micro, C + 8, qkv_cols), F32),
        ],
        compiler_params=pltpu.CompilerParams(
            dimension_semantics=("arbitrary",), vmem_limit_bytes=50 * 1024 * 1024
        ),
    )(pre, pre, pre, pre, dgated, mix, inv, upd, state, taps, small, gain)


def rms_scale(values, gain):
    return values * lax.rsqrt(jnp.mean(values * values, -1, keepdims=True) + EPS) * gain


def swish_gate(gate_val, upper_val):
    return jax.nn.silu(gate_val) * upper_val


def product(left, right):
    return jnp.dot(left, right, preferred_element_type=F32)


def outer_sum(left, right):
    return lax.dot_general(left, right, (((0,), (0,)), ((), ())), preferred_element_type=F32)


def back_through(left, right):
    return lax.dot_general(left, right, (((1,), (1,)), ((), ())), preferred_element_type=F32)


def take_rows(source, order):
    return jnp.take(source, order, axis=0)


BOTH = ("seq", "fsdp")


def body(tokens, cotangent, seq_lengths, seq_slots, norm_gain, w_query, w_key, w_value, w_decay, w_beta, w_outgate,
         query_filter, key_filter, value_filter, decay_log, decay_bias, head_gain, w_output, ffn_gain, w_gate, w_up, w_down):
    shards, groups = lax.axis_size("seq"), lax.axis_size("fsdp")
    group_pos, shard_pos = lax.axis_index("fsdp"), lax.axis_index("seq")
    micro, slots = seq_slots.shape
    width = tokens.shape[3]
    part = cotangent.shape[2]
    length = part * shards
    own = w_query.shape[0]
    heads = decay_log.shape[0] // shards
    taps_n = query_filter.shape[0]
    lanes = 128

    def by_head(weight):
        return weight.reshape(own, shards, weight.shape[1] // shards)

    def spread(columns):
        return jnp.broadcast_to(columns[:, None, :], (own, shards, columns.shape[1]))

    def filter_columns(taps):
        times = taps.shape[1] // own
        return taps.reshape(taps_n, times, own).transpose(2, 1, 0).reshape(own, times * taps_n)

    filters = jnp.concatenate([filter_columns(query_filter), filter_columns(key_filter), filter_columns(value_filter)], 1)
    extra = jnp.concatenate([norm_gain[:, None], ffn_gain[:, None], filters], 1)
    spare = lanes - 2 * heads - extra.shape[1]
    packed = jnp.concatenate(
        [by_head(w_query), by_head(w_key), by_head(w_value), by_head(w_outgate), by_head(w_decay), by_head(w_beta),
         spread(extra), jnp.zeros((own, shards, spare), BF)], 2).transpose(1, 0, 2)
    packed = lax.all_to_all(packed, "seq", split_axis=0, concat_axis=0, tiled=True)
    w_mixer = lax.all_gather(packed, "fsdp", axis=1, tiled=True).reshape(width, packed.shape[2])
    side = w_mixer[:, w_mixer.shape[1] - lanes:].astype(F32)
    at = 2 * heads
    norm_row, ffn_row = side[:, at], side[:, at + 1]
    rows_of = width // shards
    mine = lax.dynamic_slice_in_dim(side, shard_pos * rows_of, rows_of, 0)[:, at + 2:at + 2 + filters.shape[1]]

    def filter_rows(cols):
        times = cols.shape[1] // taps_n
        return cols.reshape(groups, own, times, taps_n).transpose(3, 0, 2, 1).reshape(taps_n, groups * times * own)

    taps = jnp.concatenate([filter_rows(mine[:, :taps_n]), filter_rows(mine[:, taps_n:2 * taps_n]), filter_rows(mine[:, 2 * taps_n:])], 1)
    taps = jnp.pad(taps, ((0, 8 - taps_n), (0, 0)))
    small = jnp.stack([lax.dynamic_slice_in_dim(decay_log, shard_pos * heads, heads, 0),
                       lax.dynamic_slice_in_dim(decay_bias, shard_pos * heads, heads, 0)])
    small = jnp.pad(small, ((0, 6), (0, lanes - heads)))
    gain = jnp.broadcast_to(head_gain.astype(F32)[None], (8, head_gain.shape[0]))
    w_out_t = lax.all_gather(w_output.T, BOTH, axis=0, tiled=True)
    w_ffn = lax.all_gather(jnp.stack([w_gate, w_up, w_down.T]), BOTH, axis=1, tiled=True)
    w_gate_all, w_up_all, w_down_t = w_ffn[0], w_ffn[1], w_ffn[2]

    slot_ids = jnp.arange(slots, dtype=jnp.int32)
    matches = seq_slots[:, :, None] == slot_ids[None, None, :]
    source_of = jnp.sum(jnp.where(matches, slot_ids[None, :, None], 0), axis=1)
    slot_length = jnp.sum(jnp.where(matches, seq_lengths[:, :, None], 0), axis=1)
    per_group = slots // groups
    units = micro * per_group
    local_length = lax.dynamic_slice_in_dim(slot_length, group_pos * per_group, per_group, 1).reshape(units)
    row_ids = shard_pos * part + jnp.arange(part, dtype=jnp.int32)
    valid = (row_ids[None, :] < local_length[:, None]).astype(F32)[..., None]
    ordered = jax.vmap(take_rows)(tokens, source_of)
    dealt = lax.all_to_all(ordered, "fsdp", split_axis=1, concat_axis=2, tiled=True).reshape(units, part, width)
    rows = units * part
    inputs = dealt.reshape(rows, width)
    everything = lax.all_gather(dealt, "seq", axis=1, tiled=True)

    normed = rms_scale(everything.astype(F32), norm_row).astype(BF).reshape(units * length, width)
    pre = product(normed, w_mixer).astype(BF).reshape(units, length, w_mixer.shape[1])
    gated, *saved = mixer_forward(pre, taps, small, gain, heads, shards)
    gated = lax.all_to_all(gated, "seq", split_axis=0, concat_axis=0, tiled=True)
    v_cols = gated.shape[-1]
    gated = gated.reshape(shards, rows, v_cols).transpose(1, 0, 2).reshape(rows, shards * v_cols)

    residual = inputs.astype(F32)
    attended = residual + back_through(gated, w_out_t)
    ffn_in, ffn_back = jax.vjp(rms_scale, attended, ffn_row)
    ffn_in = ffn_in.astype(BF)
    hidden, hidden_back = jax.vjp(swish_gate, product(ffn_in, w_gate_all), product(ffn_in, w_up_all))
    hidden = hidden.astype(BF)
    output = attended + back_through(hidden, w_down_t)
    mixed = (output.reshape(units, part, width) * valid).reshape(micro, per_group, part, width)
    cot = (cotangent.reshape(units, part, width).astype(F32) * valid).reshape(rows, width)
    down_in = cot.astype(BF)
    down_grad = outer_sum(down_in, hidden).astype(BF)
    gate_back, upper_back = hidden_back(product(down_in, w_down_t))
    gate_back, upper_back = gate_back.astype(BF), upper_back.astype(BF)
    gate_grad = outer_sum(ffn_in, gate_back).astype(BF)
    up_grad = outer_sum(ffn_in, upper_back).astype(BF)
    ffn_sum = lax.psum_scatter(jnp.stack([gate_grad, up_grad, down_grad]), BOTH, scatter_dimension=1, tiled=True)
    attended_back, ffn_gain_grad = ffn_back(back_through(gate_back, w_gate_all) + back_through(upper_back, w_up_all))
    attended_back = cot + attended_back
    branch_in = attended_back.astype(BF)
    output_grad = outer_sum(branch_in, gated).astype(BF)
    output_sum = lax.psum_scatter(output_grad, BOTH, scatter_dimension=0, tiled=True)
    gated_back = product(branch_in, w_out_t).astype(BF)
    gated_back = gated_back.reshape(rows, shards, v_cols).transpose(1, 0, 2).reshape(shards, units, part, v_cols)
    gated_back = lax.all_to_all(gated_back, "seq", split_axis=0, concat_axis=0, tiled=True)

    dpre, dtaps, dsmall, dgain = mixer_backward(pre, gated_back, saved, taps, small, gain, heads)
    dpre = dpre.reshape(units * length, dpre.shape[2])
    partial = back_through(dpre, w_mixer).astype(BF).reshape(units, length, width)
    normed_back = lax.psum_scatter(partial, "seq", scatter_dimension=1, tiled=True).reshape(rows, width).astype(F32)
    dw = outer_sum(normed, dpre)
    main = dw.shape[1] - lanes
    norm_gain_part = jnp.sum(dw * jnp.concatenate([w_mixer[:, :main], w_mixer[:, main:main + at], jnp.zeros((width, lanes - at), BF)], 1).astype(F32), 1) / norm_row

    def grad_columns(grads):
        times = grads.shape[1] // rows_of
        return grads.reshape(taps_n, groups, times, own).transpose(1, 3, 2, 0).reshape(rows_of, times * taps_n)

    qk_cols = heads * KD
    filter_part = jnp.concatenate([grad_columns(dtaps[:taps_n, :qk_cols]), grad_columns(dtaps[:taps_n, qk_cols:2 * qk_cols]), grad_columns(dtaps[:taps_n, 2 * qk_cols:])], 1)
    filter_part = lax.dynamic_update_slice_in_dim(jnp.zeros((width, filter_part.shape[1]), F32), filter_part, shard_pos * rows_of, 0)
    dw = jnp.concatenate([dw[:, :main + at], norm_gain_part[:, None], ffn_gain_grad[:, None], filter_part, jnp.zeros((width, spare), F32)], 1)
    dw = dw.astype(BF).reshape(shards, rows_of, dw.shape[1])
    dw = lax.psum_scatter(dw, "fsdp", scatter_dimension=1, tiled=True)
    dw = lax.all_to_all(dw, "seq", split_axis=0, concat_axis=0, tiled=True).astype(F32)

    def columns(start, stop):
        return dw[:, :, start:stop].transpose(1, 0, 2).reshape(own, shards * (stop - start))

    hv = heads * VD
    query_grad, key_grad = columns(0, qk_cols), columns(qk_cols, 2 * qk_cols)
    value_grad, outgate_grad = columns(2 * qk_cols, 2 * qk_cols + hv), columns(2 * qk_cols + hv, main)
    decay_grad, beta_grad = columns(main, main + heads), columns(main + heads, main + 2 * heads)
    gains = jnp.sum(dw[:, :, main + at:main + at + 2], 0)
    filter_own = lax.dynamic_index_in_dim(dw, shard_pos, 0, keepdims=False)[:, main + at + 2:main + at + 2 + filters.shape[1]]

    def filter_grad(cols):
        times = cols.shape[1] // taps_n
        return cols.reshape(own, times, taps_n).transpose(2, 1, 0).reshape(taps_n, times * own)

    filter_grads = (filter_grad(filter_own[:, :taps_n]), filter_grad(filter_own[:, taps_n:2 * taps_n]), filter_grad(filter_own[:, 2 * taps_n:]))

    def placed(values):
        return lax.dynamic_update_slice_in_dim(jnp.zeros(decay_log.shape, F32), values, shard_pos * heads, 0)

    decay_log_grad, decay_bias_grad, head_gain_grad = lax.psum((placed(dsmall[0, :heads]), placed(dsmall[1, :heads]), dgain[0]), BOTH)

    _, norm_back = jax.vjp(rms_scale, residual, norm_row)
    input_back, _ = norm_back(normed_back)
    slot_grad = (attended_back + input_back).astype(BF).reshape(micro, per_group, part, width)
    home = lax.all_to_all(slot_grad, "fsdp", split_axis=2, concat_axis=1, tiled=True)
    tokens_grad = jax.vmap(take_rows)(home, seq_slots).astype(F32)
    ffn_sum = ffn_sum.astype(F32)
    return (mixed, tokens_grad, gains[:, 0], query_grad, key_grad, value_grad, decay_grad, beta_grad, outgate_grad,
            *filter_grads, decay_log_grad, decay_bias_grad, head_gain_grad, output_sum.astype(F32).T, gains[:, 1],
            ffn_sum[0], ffn_sum[1], ffn_sum[2].T)


def solution(mesh):
    placed = (
        P(None, None, ("seq", "fsdp"), None),
        P(None, "fsdp", "seq", None),
        P(),
        P(),
        P(("seq", "fsdp")),
        P(("seq", "fsdp"), None),
        P(("seq", "fsdp"), None),
        P(("seq", "fsdp"), None),
        P(("seq", "fsdp"), None),
        P(("seq", "fsdp"), None),
        P(("seq", "fsdp"), None),
        P(None, ("seq", "fsdp")),
        P(None, ("seq", "fsdp")),
        P(None, ("seq", "fsdp")),
        P(),
        P(),
        P(),
        P(None, ("seq", "fsdp")),
        P(("seq", "fsdp")),
        P(("seq", "fsdp"), None),
        P(("seq", "fsdp"), None),
        P(None, ("seq", "fsdp")),
    )
    return jax.shard_map(
        body,
        mesh=mesh,
        in_specs=placed,
        out_specs=(
            P(None, "fsdp", "seq", None),
            P(None, None, ("seq", "fsdp"), None),
            P(("seq", "fsdp")),
            P(("seq", "fsdp"), None),
            P(("seq", "fsdp"), None),
            P(("seq", "fsdp"), None),
            P(("seq", "fsdp"), None),
            P(("seq", "fsdp"), None),
            P(("seq", "fsdp"), None),
            P(None, ("seq", "fsdp")),
            P(None, ("seq", "fsdp")),
            P(None, ("seq", "fsdp")),
            P(),
            P(),
            P(),
            P(None, ("seq", "fsdp")),
            P(("seq", "fsdp")),
            P(("seq", "fsdp"), None),
            P(("seq", "fsdp"), None),
            P(None, ("seq", "fsdp")),
        ),
        check_vma=False,
    )
```

```python
import functools
import jax
import jax.numpy as jnp
from jax import lax
from jax.experimental import pallas as pl
from jax.experimental.pallas import tpu as pltpu
from jax.sharding import PartitionSpec as P

EPS = 1e-6
C = 128
KD = 128
VD = 256
F32 = jnp.float32
BF = jnp.bfloat16
HIGHEST = lax.Precision.HIGHEST

def iota(shape, dim):
    return lax.broadcasted_iota(jnp.int32, shape, dim)

def mm(a, b, ca=1, cb=0):
    return lax.dot_general(a.astype(BF), b.astype(BF), (((ca,), (cb,)), ((), ())), preferred_element_type=F32)

def exact(a, b):
    return lax.dot_general(a, b, (((1,), (0,)), ((), ())), precision=HIGHEST, preferred_element_type=F32)

def unit_inverse(low):
    rows, cols = iota((C, C), 0), iota((C, C), 1)
    diag = jnp.where(rows // 16 == cols // 16, low, 0.0)
    packed = jnp.sum(diag.reshape(C // 16, 16, C), axis=0)
    prow, pcol = iota((16, C), 0), iota((16, C), 1)
    inv = jnp.where(prow == pcol % 16, 1.0, 0.0).astype(F32)
    base = (pcol // 16) * 16
    for j in range(15):
        col = jnp.take_along_axis(packed, base + j, axis=1)
        inv = inv - col * inv[j:j + 1, :]
    full = jnp.broadcast_to(inv[None], (C // 16, 16, C)).reshape(C, C)
    full = jnp.where(rows // 16 == cols // 16, full, 0.0)
    size = 16
    while size < C:
        off = jnp.where((rows // (2 * size) == cols // (2 * size)) & (rows // size == cols // size + 1), low, 0.0)
        full = full - mm(mm(full, off), full)
        size *= 2
    return full

def gates(pre, dlog, dbias):
    arg = pre + dbias
    soft = jnp.maximum(arg, 0.0) + jnp.log1p(jnp.exp(-jnp.abs(arg)))
    log_decay = -jnp.exp(dlog) * soft
    rows, cols = iota((C, C), 0), iota((C, C), 1)
    tri = jnp.where(rows >= cols, 1.0, 0.0).astype(F32)
    cum = exact(tri, log_decay)
    return log_decay, cum

def sig(x):
    return 1.0 / (1.0 + jnp.exp(-x))

def conv_taps(ext_ref, taps, width):
    acc = ext_ref[pl.ds(5, C), :] * taps[0:1, :]
    for i in range(1, 4):
        acc = acc + ext_ref[pl.ds(5 + i, C), :] * taps[i:i + 1, :]
    return acc

def load_ext(qkv, halo, ext_ref, first):
    ahead = halo[8:16, :].astype(F32)
    ext_ref[pl.ds(0, 8), :] = jnp.where(first, 0.0, ahead)
    ext_ref[pl.ds(8, C), :] = qkv.astype(F32)

def forward_kernel(heads, micro, qkv_ref, halo_ref, og_ref, db_ref, taps_ref, small_ref, gain_ref,
                   gated_ref, mix_ref, inv_ref, upd_ref, state_ref, mem_ref, ext_ref):
    step = pl.program_id(0)
    first = step == 0

    @pl.when(first)
    def _():
        mem_ref[...] = jnp.zeros_like(mem_ref)

    taps = taps_ref[...]
    rows, cols = iota((C, C), 0), iota((C, C), 1)
    lower = rows >= cols
    gain = gain_ref[0:1, :]
    for m in range(micro):
        ext = ext_ref.at[m]
        load_ext(qkv_ref[m], halo_ref[m], ext, first)
        act = conv_taps(ext, taps, None)
        act = act * sig(act)
        pre = db_ref[m].astype(F32)
        _, cum = gates(pre, small_ref[0:1, :], small_ref[1:2, :])
        rate = sig(pre)
        cum_t = jnp.transpose(cum)
        for h in range(heads):
            u = m * heads + h
            q = act[:, h * KD:(h + 1) * KD]
            k = act[:, (heads + h) * KD:(heads + h + 1) * KD]
            v = act[:, 2 * heads * KD + h * VD:2 * heads * KD + (h + 1) * VD]
            q = q * (lax.rsqrt(jnp.sum(q * q, -1, keepdims=True) + EPS) * KD ** -0.5)
            k = k * lax.rsqrt(jnp.sum(k * k, -1, keepdims=True) + EPS)
            beta = rate[:, heads + h:heads + h + 1]
            gcol = cum[:, h:h + 1]
            grow = cum_t[h:h + 1, :]
            decay = jnp.where(lower, jnp.exp(jnp.where(lower, gcol - grow, 0.0)), 0.0)
            grow_col = jnp.exp(gcol)
            glast = cum[C - 1:C, h:h + 1]
            dots = mm(jnp.concatenate([k, q], 0), k, 1, 1)
            low = jnp.where(rows > cols, beta * decay * dots[:C], 0.0)
            scores = decay * dots[C:]
            inv = unit_inverse(low)
            mem = mem_ref[u]
            state_ref[0, u] = mem.astype(state_ref.dtype)
            from_mem = mm(jnp.concatenate([grow_col * k, grow_col * q], 0), mem)
            upd = mm(inv, beta * (v - from_mem[:C]))
            out = from_mem[C:] + mm(scores, upd)
            mem_ref[u] = jnp.exp(glast) * mem + mm(k * jnp.exp(glast - gcol), upd, 0, 0)
            inv_ref[0, u] = inv.astype(inv_ref.dtype)
            upd_ref[0, u] = upd.astype(upd_ref.dtype)
            mix = out.astype(BF)
            mix_ref[0, u] = mix
            mix = mix.astype(F32)
            og = og_ref[m, :, h * VD:(h + 1) * VD].astype(F32)
            scale = lax.rsqrt(jnp.mean(mix * mix, -1, keepdims=True) + EPS)
            gated = mix * scale * gain * (og * sig(og))
            gated_ref[0, m, :, h * VD:(h + 1) * VD] = gated.astype(BF)


def mixer_forward(pre, taps, small, gain, heads, shards):
    micro, length, _ = pre.shape
    count = length // C
    units = micro * heads
    qkv_cols, v_cols = heads * (2 * KD + VD), heads * VD
    per = count // shards
    lead = (2 * heads * KD + 2 * v_cols) // 128
    return pl.pallas_call(
        functools.partial(forward_kernel, heads, micro),
        grid=(count,),
        in_specs=[
            pl.BlockSpec((micro, C, qkv_cols), lambda c: (0, c, 0)),
            pl.BlockSpec((micro, 16, qkv_cols), lambda c: (0, jnp.maximum(c * (C // 16) - 1, 0), 0)),
            pl.BlockSpec((micro, C, v_cols), lambda c: (0, c, 2)),
            pl.BlockSpec((micro, C, 128), lambda c: (0, c, lead + 0)),
            pl.BlockSpec((8, qkv_cols), lambda c: (0, 0)),
            pl.BlockSpec((8, 128), lambda c: (0, 0)),
            pl.BlockSpec((8, VD), lambda c: (0, 0)),
        ],
        out_specs=[
            pl.BlockSpec((1, micro, C, v_cols), lambda c: (c // per, 0, c % per, 0)),
            pl.BlockSpec((1, units, C, VD), lambda c: (c, 0, 0, 0)),
            pl.BlockSpec((1, units, C, C), lambda c: (c, 0, 0, 0)),
            pl.BlockSpec((1, units, C, VD), lambda c: (c, 0, 0, 0)),
            pl.BlockSpec((1, units, KD, VD), lambda c: (c, 0, 0, 0)),
        ],
        out_shape=[
            jax.ShapeDtypeStruct((shards, micro, length // shards, v_cols), BF),
            jax.ShapeDtypeStruct((count, units, C, VD), BF),
            jax.ShapeDtypeStruct((count, units, C, C), BF),
            jax.ShapeDtypeStruct((count, units, C, VD), BF),
            jax.ShapeDtypeStruct((count, units, KD, VD), BF),
        ],
        scratch_shapes=[
            pltpu.VMEM((units, KD, VD), F32),
            pltpu.VMEM((micro, C + 8, qkv_cols), F32),
        ],
        compiler_params=pltpu.CompilerParams(
            dimension_semantics=("arbitrary",), vmem_limit_bytes=50 * 1024 * 1024
        ),
    )(pre, pre, pre, pre, taps, small, gain)


def backward_kernel(heads, micro, qkv_ref, halo_ref, og_ref, db_ref, dgated_ref, mix_ref, inv_ref, upd_ref, state_ref,
                    taps_ref, small_ref, gain_ref,
                    dpre_ref, dtaps_ref, dsmall_ref, dgain_ref, dmem_ref, ext_ref, dy_ref):
    step = pl.program_id(0)
    count = pl.num_programs(0)

    @pl.when(step == 0)
    def _():
        dmem_ref[...] = jnp.zeros_like(dmem_ref)
        dtaps_ref[...] = jnp.zeros_like(dtaps_ref)
        dsmall_ref[...] = jnp.zeros_like(dsmall_ref)
        dgain_ref[...] = jnp.zeros_like(dgain_ref)

    taps = taps_ref[...]
    rows, cols = iota((C, C), 0), iota((C, C), 1)
    lower = rows >= cols
    upper = jnp.where(rows <= cols, 1.0, 0.0).astype(F32)
    gain = gain_ref[0:1, :]
    qk_cols = heads * KD
    for m in range(micro):
        ext, dy = ext_ref.at[m], dy_ref.at[m]
        load_ext(qkv_ref[m], halo_ref[m], ext, step == count - 1)
        dy[pl.ds(C, 8), :] = jnp.where(step == 0, 0.0, dy[pl.ds(0, 8), :])
        conv = conv_taps(ext, taps, None)
        gate = sig(conv)
        act = conv * gate
        dgate = gate * (1.0 + conv * (1.0 - gate))
        pre = db_ref[m].astype(F32)
        log_decay, cum = gates(pre, small_ref[0:1, :], small_ref[1:2, :])
        rate = sig(pre)
        cum_t = jnp.transpose(cum)
        dcum = jnp.zeros((C, 128), F32)
        drate = jnp.zeros((C, 128), F32)
        for h in range(heads):
            u = m * heads + h
            q0 = act[:, h * KD:(h + 1) * KD]
            k0 = act[:, qk_cols + h * KD:qk_cols + (h + 1) * KD]
            v = act[:, 2 * qk_cols + h * VD:2 * qk_cols + (h + 1) * VD]
            qr = lax.rsqrt(jnp.sum(q0 * q0, -1, keepdims=True) + EPS)
            kr = lax.rsqrt(jnp.sum(k0 * k0, -1, keepdims=True) + EPS)
            qn, k = q0 * qr, k0 * kr
            q = qn * KD ** -0.5
            beta = rate[:, heads + h:heads + h + 1]
            gcol = cum[:, h:h + 1]
            grow = cum_t[h:h + 1, :]
            decay = jnp.where(lower, jnp.exp(jnp.where(lower, gcol - grow, 0.0)), 0.0)
            growth = jnp.exp(gcol)
            glast = cum[C - 1:C, h:h + 1]
            tail = jnp.exp(glast - gcol)
            dots = mm(jnp.concatenate([k, q], 0), k, 1, 1)
            near = jnp.where(rows > cols, decay * dots[:C], 0.0)
            scores = decay * dots[C:]
            mix = mix_ref[0, u].astype(F32)
            og = og_ref[m, :, h * VD:(h + 1) * VD].astype(F32)
            dgated = dgated_ref[0, m, :, h * VD:(h + 1) * VD].astype(F32)
            scale = lax.rsqrt(jnp.mean(mix * mix, -1, keepdims=True) + EPS)
            mixn = mix * scale
            osig = sig(og)
            dog = dgated * mixn * gain * (osig * (1.0 + og * (1.0 - osig)))
            dn = dgated * (og * osig)
            dgain_ref[0:1, :] += jnp.sum(dn * mixn, 0, keepdims=True)
            dn = dn * gain
            dout = scale * (dn - mixn * jnp.mean(dn * mixn, -1, keepdims=True))
            dout = dout.astype(BF)
            upd, mem, inv, dmem = upd_ref[0, u], state_ref[0, u], inv_ref[0, u], dmem_ref[u]
            dmem_low = dmem.astype(BF)
            both = jnp.concatenate([upd, mem], 0)
            one = mm(dout, both, 1, 1)
            dscores = jnp.where(lower, one[:, :C], 0.0)
            dq_in = one[:, C:]
            ktail = k * tail
            dupd = mm(scores, dout, 0, 0) + mm(ktail, dmem_low)
            dres = mm(inv, dupd, 0, 0)
            two = mm(dres, both, 1, 1)
            dlow = jnp.where(rows > cols, -two[:, :C], 0.0)
            dk_in = two[:, C:]
            kin, qin = growth * k, growth * q
            dk_scaled = -beta * dk_in
            dmem_new = jnp.exp(glast) * dmem + mm(qin, dout, 0, 0) - mm(beta * kin, dres, 0, 0)
            dk_tail = mm(upd, dmem_low, 1, 1)
            pull = dscores * scores
            pull_low = dlow * near
            pulls = pull + beta * pull_low
            in_parts = jnp.sum(dq_in * qin + dk_scaled * kin - dk_tail * ktail + pulls, -1, keepdims=True)
            tail_sum = jnp.sum(jnp.sum(dk_tail * ktail, -1, keepdims=True), 0, keepdims=True)
            mem_sum = jnp.sum(jnp.sum(dmem * mem.astype(F32), -1, keepdims=True), 0, keepdims=True)
            dcum_col = in_parts - jnp.transpose(jnp.broadcast_to(jnp.sum(pulls, 0, keepdims=True), (C, C)))[:, 0:1]
            last = iota((C, 1), 0) == C - 1
            dcum_col = dcum_col + jnp.where(last, tail_sum + jnp.exp(glast) * mem_sum, 0.0)
            dbeta = jnp.sum(dres * v, -1, keepdims=True) + jnp.sum(pull_low - dk_in * kin, -1, keepdims=True)
            lane = iota((C, 128), 1)
            dcum = jnp.where(lane == h, dcum_col, dcum)
            drate = jnp.where(lane == heads + h, dbeta, drate)
            dqk = dscores * decay
            dkk = dlow * decay * beta
            left = mm(jnp.concatenate([dqk, dkk], 0), k)
            dq = left[:C] + growth * dq_in
            dk = left[C:] + mm(dqk, q, 0, 0) + mm(dkk, k, 0, 0) + growth * dk_scaled + tail * dk_tail
            dv = beta * dres
            dmem_ref[u] = dmem_new
            dq = dq * KD ** -0.5
            dq = qr * (dq - qn * jnp.sum(dq * qn, -1, keepdims=True))
            dk = kr * (dk - k * jnp.sum(dk * k, -1, keepdims=True))
            for part, at, wide in ((dq, h * KD, KD), (dk, qk_cols + h * KD, KD), (dv, 2 * qk_cols + h * VD, VD)):
                dy[pl.ds(0, C), at:at + wide] = part * dgate[:, at:at + wide]
            at = 2 * qk_cols + heads * VD + h * VD
            dpre_ref[m, :, at:at + VD] = dog.astype(BF)
        grad = dy[pl.ds(0, C), :]
        dx = dy[pl.ds(3, C), :] * taps[0:1, :]
        for i in range(1, 4):
            dx = dx + dy[pl.ds(3 - i, C), :] * taps[i:i + 1, :]
        dpre_ref[m, :, 0:2 * qk_cols + heads * VD] = dx.astype(BF)
        for i in range(4):
            dtaps_ref[i:i + 1, :] += jnp.sum(grad * ext[pl.ds(5 + i, C), :], 0, keepdims=True)
        dlog = exact(upper, dcum)
        speed = -jnp.exp(small_ref[0:1, :])
        ddecay = dlog * speed * sig(pre + small_ref[1:2, :])
        dsmall_ref[0:1, :] += jnp.sum(dlog * log_decay, 0, keepdims=True)
        dsmall_ref[1:2, :] += jnp.sum(ddecay, 0, keepdims=True)
        ddb = ddecay + drate * rate * (1.0 - rate)
        at = 2 * qk_cols + 2 * heads * VD
        dpre_ref[m, :, at:at + 128] = ddb.astype(BF)


def mixer_backward(pre, dgated, saved, taps, small, gain, heads):
    mix, inv, upd, state = saved
    shards, micro, part, v_cols = dgated.shape
    length, width = pre.shape[1:]
    count = length // C
    units = micro * heads
    qkv_cols = heads * (2 * KD + VD)
    per = count // shards
    lead = (2 * heads * KD + 2 * v_cols) // 128
    end = count - 1
    keep = lambda *s: pl.BlockSpec((1, units) + s, lambda c: (end - c, 0, 0, 0))
    return pl.pallas_call(
        functools.partial(backward_kernel, heads, micro),
        grid=(count,),
        in_specs=[
            pl.BlockSpec((micro, C, qkv_cols), lambda c: (0, end - c, 0)),
            pl.BlockSpec((micro, 16, qkv_cols), lambda c: (0, jnp.maximum((end - c) * (C // 16) - 1, 0), 0)),
            pl.BlockSpec((micro, C, v_cols), lambda c: (0, end - c, 2)),
            pl.BlockSpec((micro, C, 128), lambda c: (0, end - c, lead)),
            pl.BlockSpec((1, micro, C, v_cols), lambda c: ((end - c) // per, 0, (end - c) % per, 0)),
            keep(C, VD), keep(C, C), keep(C, VD), keep(KD, VD),
            pl.BlockSpec((8, qkv_cols), lambda c: (0, 0)),
            pl.BlockSpec((8, 128), lambda c: (0, 0)),
            pl.BlockSpec((8, VD), lambda c: (0, 0)),
        ],
        out_specs=[
            pl.BlockSpec((micro, C, width), lambda c: (0, end - c, 0)),
            pl.BlockSpec((8, qkv_cols), lambda c: (0, 0)),
            pl.BlockSpec((8, 128), lambda c: (0, 0)),
            pl.BlockSpec((8, VD), lambda c: (0, 0)),
        ],
        out_shape=[
            jax.ShapeDtypeStruct((micro, length, width), BF),
            jax.ShapeDtypeStruct((8, qkv_cols), F32),
            jax.ShapeDtypeStruct((8, 128), F32),
            jax.ShapeDtypeStruct((8, VD), F32),
        ],
        scratch_shapes=[
            pltpu.VMEM((units, KD, VD), F32),
            pltpu.VMEM((micro, C + 8, qkv_cols), F32),
            pltpu.VMEM((micro, C + 8, qkv_cols), F32),
        ],
        compiler_params=pltpu.CompilerParams(
            dimension_semantics=("arbitrary",), vmem_limit_bytes=50 * 1024 * 1024
        ),
    )(pre, pre, pre, pre, dgated, mix, inv, upd, state, taps, small, gain)


MESH_ID = pl.DeviceIdType.MESH


def start_kernel(shards, groups, rows_y, micro, tok_ref, pack_ref, every_ref, wm_ref,
                 local_sem, send_sem, one_sem, z_sem, y_sem, deal_sem, swap_sem):
    s, f = lax.axis_index("seq"), lax.axis_index("fsdp")
    deep = groups // rows_y
    z, y = f // rows_y, lax.rem(f, rows_y)
    barrier = pltpu.get_barrier_semaphore()
    for d in range(1, shards):
        pl.semaphore_signal(barrier, inc=1, device_id=(jnp.bitwise_xor(s, d), f), device_id_type=MESH_ID)
    for k in range(1, groups):
        pl.semaphore_signal(barrier, inc=1, device_id=(s, lax.rem(f + k, groups)), device_id_type=MESH_ID)
    pl.semaphore_wait(barrier, shards + groups - 2)

    sent = []

    def send(src, dst, sem, device):
        at = len(sent)
        copy = pltpu.make_async_remote_copy(src, dst, send_sem.at[at], sem, device_id=device, device_id_type=MESH_ID)
        copy.start()
        sent.append(copy)
        return copy

    place = wm_ref.at[s, z, y]
    first = []
    for d in range(1, shards):
        to = jnp.bitwise_xor(s, d)
        first.append(send(pack_ref.at[to], place, one_sem.at[d], (to, f)))
    mine = pltpu.make_async_copy(pack_ref.at[s], place, local_sem.at[0])
    mine.start()
    keeps = []
    for m in range(micro):
        keep = pltpu.make_async_copy(tok_ref.at[m, f], every_ref.at[m, s, f], local_sem.at[1 + m])
        keep.start()
        keeps.append(keep)

    def deal(m):
        return [send(tok_ref.at[m, lax.rem(f + k, groups)], every_ref.at[m, s, f], deal_sem.at[m, k],
                     (s, lax.rem(f + k, groups))) for k in range(1, groups)]

    dealt = [deal(0)]
    columns = []
    mine.wait()
    for d in range(shards):
        block = jnp.bitwise_xor(s, d)
        if d:
            first[d - 1].wait_recv()
        columns.append([send(wm_ref.at[block, z, y], wm_ref.at[block, z, y], z_sem.at[d, k],
                             (s, lax.rem(z + k, deep) * rows_y + y)) for k in range(1, deep)])
    for m in range(1, micro):
        dealt.append(deal(m))

    bits = []
    bit = shards // 2
    while bit:
        bits.append(bit)
        bit //= 2

    def swap(m, level):
        bit = bits[level]
        held = [0]
        for b in bits[:level]:
            held = held + [h | b for h in held]
        return [send(every_ref.at[m, jnp.bitwise_xor(s, h)], every_ref.at[m, jnp.bitwise_xor(s, h)],
                     swap_sem.at[m, level, i], (jnp.bitwise_xor(s, bit), f)) for i, h in enumerate(held)]

    rows_of = []
    swaps = {}
    for m in range(micro):
        keeps[m].wait()
        for copy in dealt[m]:
            copy.wait_recv()
        swaps[m, 0] = swap(m, 0)
        if m == 0:
            for d in range(shards):
                block = jnp.bitwise_xor(s, d)
                for copy in columns[d]:
                    copy.wait_recv()
                rows_of.append([send(wm_ref.at[block, :, y], wm_ref.at[block, :, y], y_sem.at[d, j],
                                     (s, z * rows_y + lax.rem(y + j, rows_y))) for j in range(1, rows_y)])
    for level in range(1, len(bits)):
        for m in range(micro):
            for copy in swaps[m, level - 1]:
                copy.wait_recv()
            swaps[m, level] = swap(m, level)
    for m in range(micro):
        for copy in swaps[m, len(bits) - 1]:
            copy.wait_recv()
    for d in range(shards):
        for copy in rows_of[d]:
            copy.wait_recv()
    for copy in sent:
        copy.wait_send()


def start_exchange(tok, pack, shards, groups):
    micro, _, own, width = tok.shape
    rows_y = max(shards // 2, 1)
    deep = groups // rows_y
    levels = max(shards.bit_length() - 1, 1)
    copies = (shards - 1) + micro * (groups - 1) + shards * (deep - 1) + shards * (rows_y - 1) + micro * (shards - 1)
    hbm = pl.BlockSpec(memory_space=pl.ANY)
    return pl.pallas_call(
        functools.partial(start_kernel, shards, groups, rows_y, micro),
        in_specs=[hbm, hbm],
        out_specs=[hbm, hbm],
        out_shape=[
            jax.ShapeDtypeStruct((micro, shards, groups, own, width), tok.dtype),
            jax.ShapeDtypeStruct((shards, deep, rows_y) + pack.shape[1:], pack.dtype),
        ],
        scratch_shapes=[
            pltpu.SemaphoreType.DMA((1 + micro,)),
            pltpu.SemaphoreType.DMA((copies,)),
            pltpu.SemaphoreType.DMA((shards,)),
            pltpu.SemaphoreType.DMA((shards, deep)),
            pltpu.SemaphoreType.DMA((shards, rows_y)),
            pltpu.SemaphoreType.DMA((micro, groups)),
            pltpu.SemaphoreType.DMA((micro, levels, max(shards // 2, 1))),
        ],
        compiler_params=pltpu.CompilerParams(collective_id=0, has_side_effects=True),
    )(tok, pack)


def rms_scale(values, gain):
    return values * lax.rsqrt(jnp.mean(values * values, -1, keepdims=True) + EPS) * gain


def swish_gate(gate_val, upper_val):
    return jax.nn.silu(gate_val) * upper_val


def product(left, right):
    return jnp.dot(left, right, preferred_element_type=F32)


def outer_sum(left, right):
    return lax.dot_general(left, right, (((0,), (0,)), ((), ())), preferred_element_type=F32)


def back_through(left, right):
    return lax.dot_general(left, right, (((1,), (1,)), ((), ())), preferred_element_type=F32)


def take_rows(source, order):
    return jnp.take(source, order, axis=0)


BOTH = ("seq", "fsdp")


def bits_of(size):
    return [1 << i for i in reversed(range(size.bit_length() - 1))]


def reduce_halves(values, names, sizes, order):
    left = [(name, bit) for name, size in zip(names, sizes) for bit in bits_of(size)]
    values = values.reshape((2,) * len(left) + values.shape[len(names):])
    for name, bit in order:
        at = left.index((name, bit))
        side = (lax.axis_index(name) // bit) % 2
        away = lax.dynamic_index_in_dim(values, 1 - side, at, keepdims=False)
        kept = lax.dynamic_index_in_dim(values, side, at, keepdims=False)
        came = lax.ppermute(away, name, [(i, i ^ bit) for i in range(sizes[names.index(name)])])
        values = kept.astype(F32) + came.astype(F32)
        left.pop(at)
        if left:
            values = values.astype(BF)
    return values


def body(tokens, cotangent, seq_lengths, seq_slots, norm_gain, w_query, w_key, w_value, w_decay, w_beta, w_outgate,
         query_filter, key_filter, value_filter, decay_log, decay_bias, head_gain, w_output, ffn_gain, w_gate, w_up, w_down):
    shards, groups = lax.axis_size("seq"), lax.axis_size("fsdp")
    group_pos, shard_pos = lax.axis_index("fsdp"), lax.axis_index("seq")
    micro, slots = seq_slots.shape
    width = tokens.shape[3]
    part = cotangent.shape[2]
    length = part * shards
    own = w_query.shape[0]
    heads = decay_log.shape[0] // shards
    taps_n = query_filter.shape[0]
    lanes = 128

    def by_head(weight):
        return weight.reshape(own, shards, weight.shape[1] // shards)

    def spread(columns):
        return jnp.broadcast_to(columns[:, None, :], (own, shards, columns.shape[1]))

    def filter_columns(taps):
        times = taps.shape[1] // own
        return taps.reshape(taps_n, times, own).transpose(2, 1, 0).reshape(own, times * taps_n)

    filters = jnp.concatenate([filter_columns(query_filter), filter_columns(key_filter), filter_columns(value_filter)], 1)
    extra = jnp.concatenate([norm_gain[:, None], ffn_gain[:, None], filters], 1)
    spare = lanes - 2 * heads - extra.shape[1]
    packed = jnp.concatenate(
        [by_head(w_query), by_head(w_key), by_head(w_value), by_head(w_outgate), by_head(w_decay), by_head(w_beta),
         spread(extra), jnp.zeros((own, shards, spare), BF)], 2).transpose(1, 0, 2)

    slot_ids = jnp.arange(slots, dtype=jnp.int32)
    matches = seq_slots[:, :, None] == slot_ids[None, None, :]
    source_of = jnp.sum(jnp.where(matches, slot_ids[None, :, None], 0), axis=1)
    slot_length = jnp.sum(jnp.where(matches, seq_lengths[:, :, None], 0), axis=1)
    units = micro
    local_length = lax.dynamic_slice_in_dim(slot_length, group_pos, 1, 1).reshape(units)
    row_ids = shard_pos * part + jnp.arange(part, dtype=jnp.int32)
    valid = (row_ids[None, :] < local_length[:, None]).astype(F32)[..., None]
    ordered = jax.vmap(take_rows)(tokens, source_of)
    everything, w_mixer = start_exchange(ordered, packed, shards, groups)
    everything = everything.reshape(units, length, width)
    w_mixer = w_mixer.reshape(width, packed.shape[2])
    rows = units * part
    inputs = lax.dynamic_slice_in_dim(everything, shard_pos * part, part, 1).reshape(rows, width)
    side = w_mixer[:, w_mixer.shape[1] - lanes:].astype(F32)
    at = 2 * heads
    norm_row, ffn_row = side[:, at], side[:, at + 1]
    rows_of = width // shards
    mine = lax.dynamic_slice_in_dim(side, shard_pos * rows_of, rows_of, 0)[:, at + 2:at + 2 + filters.shape[1]]

    def filter_rows(cols):
        times = cols.shape[1] // taps_n
        return cols.reshape(groups, own, times, taps_n).transpose(3, 0, 2, 1).reshape(taps_n, groups * times * own)

    taps = jnp.concatenate([filter_rows(mine[:, :taps_n]), filter_rows(mine[:, taps_n:2 * taps_n]), filter_rows(mine[:, 2 * taps_n:])], 1)
    taps = jnp.pad(taps, ((0, 8 - taps_n), (0, 0)))
    small = jnp.stack([lax.dynamic_slice_in_dim(decay_log, shard_pos * heads, heads, 0),
                       lax.dynamic_slice_in_dim(decay_bias, shard_pos * heads, heads, 0)])
    small = jnp.pad(small, ((0, 6), (0, lanes - heads)))
    gain = jnp.broadcast_to(head_gain.astype(F32)[None], (8, head_gain.shape[0]))
    dense = jnp.concatenate([w_gate, w_up, w_down.T, w_output.T], 1)
    dense, everything = lax.optimization_barrier((dense, everything))
    w_dense = lax.all_gather(dense, BOTH, axis=0, tiled=True)
    hidden_n = w_gate.shape[1]
    w_gate_all, w_up_all = w_dense[:, :hidden_n], w_dense[:, hidden_n:2 * hidden_n]
    w_down_t, w_out_t = w_dense[:, 2 * hidden_n:3 * hidden_n], w_dense[:, 3 * hidden_n:]

    normed = rms_scale(everything.astype(F32), norm_row).astype(BF).reshape(units * length, width)
    pre = product(normed, w_mixer).astype(BF).reshape(units, length, w_mixer.shape[1])
    gated, *saved = mixer_forward(pre, taps, small, gain, heads, shards)
    gated = lax.all_to_all(gated, "seq", split_axis=0, concat_axis=0, tiled=True)
    v_cols = gated.shape[-1]
    gated = gated.reshape(shards, rows, v_cols).transpose(1, 0, 2).reshape(rows, shards * v_cols)

    residual = inputs.astype(F32)
    attended = residual + back_through(gated, w_out_t)
    ffn_in, ffn_back = jax.vjp(rms_scale, attended, ffn_row)
    ffn_in = ffn_in.astype(BF)
    hidden, hidden_back = jax.vjp(swish_gate, product(ffn_in, w_gate_all), product(ffn_in, w_up_all))
    hidden = hidden.astype(BF)
    output = attended + back_through(hidden, w_down_t)
    mixed = (output.reshape(units, part, width) * valid).reshape(micro, 1, part, width)
    cot = (cotangent.reshape(units, part, width).astype(F32) * valid).reshape(rows, width)
    down_in = cot.astype(BF)
    down_grad = outer_sum(down_in, hidden).astype(BF)
    gate_back, upper_back = hidden_back(product(down_in, w_down_t))
    gate_back, upper_back = gate_back.astype(BF), upper_back.astype(BF)
    gate_grad = outer_sum(ffn_in, gate_back).astype(BF)
    up_grad = outer_sum(ffn_in, upper_back).astype(BF)
    attended_back, ffn_gain_grad = ffn_back(back_through(gate_back, w_gate_all) + back_through(upper_back, w_up_all))
    attended_back = cot + attended_back
    branch_in = attended_back.astype(BF)
    output_grad = outer_sum(branch_in, gated).astype(BF)
    dense_grad = jnp.concatenate([gate_grad, up_grad, down_grad], 1)
    gated_back = product(branch_in, w_out_t).astype(BF)
    gated_back = gated_back.reshape(rows, shards, v_cols).transpose(1, 0, 2).reshape(shards, units, part, v_cols)
    gated_back = lax.all_to_all(gated_back, "seq", split_axis=0, concat_axis=0, tiled=True)

    gated_back, dense_grad, output_grad = lax.optimization_barrier((gated_back, dense_grad, output_grad))
    dense_sum = lax.psum_scatter(dense_grad, BOTH, scatter_dimension=0, tiled=True)
    seq_order = [("seq", bit) for bit in reversed(bits_of(shards))]
    group_order = [("fsdp", bit) for bit in reversed(bits_of(groups))]
    output_sum = reduce_halves(output_grad.reshape(shards, groups, own, output_grad.shape[1]), BOTH, (shards, groups), seq_order + group_order)

    dpre, dtaps, dsmall, dgain = mixer_backward(pre, gated_back, saved, taps, small, gain, heads)
    dpre = dpre.reshape(units * length, dpre.shape[2])
    partial = back_through(dpre, w_mixer).astype(BF).reshape(units, shards, part, width)
    normed_back = reduce_halves(partial.transpose(1, 0, 2, 3), ("seq",), (shards,), seq_order).reshape(rows, width)
    dw = outer_sum(normed, dpre)
    main = dw.shape[1] - lanes
    norm_gain_part = jnp.sum(dw * jnp.concatenate([w_mixer[:, :main], w_mixer[:, main:main + at], jnp.zeros((width, lanes - at), BF)], 1).astype(F32), 1) / norm_row

    def grad_columns(grads):
        times = grads.shape[1] // rows_of
        return grads.reshape(taps_n, groups, times, own).transpose(1, 3, 2, 0).reshape(rows_of, times * taps_n)

    qk_cols = heads * KD
    filter_part = jnp.concatenate([grad_columns(dtaps[:taps_n, :qk_cols]), grad_columns(dtaps[:taps_n, qk_cols:2 * qk_cols]), grad_columns(dtaps[:taps_n, 2 * qk_cols:])], 1)
    filter_part = lax.dynamic_update_slice_in_dim(jnp.zeros((width, filter_part.shape[1]), F32), filter_part, shard_pos * rows_of, 0)
    dw = jnp.concatenate([dw[:, :main + at], norm_gain_part[:, None], ffn_gain_grad[:, None], filter_part, jnp.zeros((width, spare), F32)], 1)
    dw = dw.astype(BF).reshape(shards, groups, own, dw.shape[1])
    half = shards // 2
    turned = group_order[1:2] + group_order[:1] + group_order[2:]
    dw = jnp.concatenate([reduce_halves(dw[:half].transpose(1, 0, 2, 3), ("fsdp",), (groups,), group_order),
                          reduce_halves(dw[half:].transpose(1, 0, 2, 3), ("fsdp",), (groups,), turned)]).astype(BF)
    dw = lax.all_to_all(dw, "seq", split_axis=0, concat_axis=0, tiled=True).astype(F32)

    def columns(start, stop):
        return dw[:, :, start:stop].transpose(1, 0, 2).reshape(own, shards * (stop - start))

    hv = heads * VD
    query_grad, key_grad = columns(0, qk_cols), columns(qk_cols, 2 * qk_cols)
    value_grad, outgate_grad = columns(2 * qk_cols, 2 * qk_cols + hv), columns(2 * qk_cols + hv, main)
    decay_grad, beta_grad = columns(main, main + heads), columns(main + heads, main + 2 * heads)
    gains = jnp.sum(dw[:, :, main + at:main + at + 2], 0)
    filter_own = lax.dynamic_index_in_dim(dw, shard_pos, 0, keepdims=False)[:, main + at + 2:main + at + 2 + filters.shape[1]]

    def filter_grad(cols):
        times = cols.shape[1] // taps_n
        return cols.reshape(own, times, taps_n).transpose(2, 1, 0).reshape(taps_n, times * own)

    filter_grads = (filter_grad(filter_own[:, :taps_n]), filter_grad(filter_own[:, taps_n:2 * taps_n]), filter_grad(filter_own[:, 2 * taps_n:]))

    def placed(values):
        return lax.dynamic_update_slice_in_dim(jnp.zeros(decay_log.shape, F32), values, shard_pos * heads, 0)

    little = jnp.concatenate([placed(dsmall[0, :heads]), placed(dsmall[1, :heads]), dgain[0]])
    devices = shards * groups
    little = lax.all_to_all(jnp.broadcast_to(little[None], (devices, little.shape[0])), BOTH, split_axis=0, concat_axis=0, tiled=True)
    little = jnp.sum(little, 0)
    count = decay_log.shape[0]
    decay_log_grad, decay_bias_grad, head_gain_grad = little[:count], little[count:2 * count], little[2 * count:]

    _, norm_back = jax.vjp(rms_scale, residual, norm_row)
    input_back, _ = norm_back(normed_back)
    slot_grad = (attended_back + input_back).astype(BF).reshape(micro, 1, part, width)
    home = lax.all_to_all(slot_grad, "fsdp", split_axis=2, concat_axis=1, tiled=True)
    tokens_grad = jax.vmap(take_rows)(home, seq_slots).astype(F32)
    dense_sum = dense_sum.astype(F32)
    return (mixed, tokens_grad, gains[:, 0], query_grad, key_grad, value_grad, decay_grad, beta_grad, outgate_grad,
            *filter_grads, decay_log_grad, decay_bias_grad, head_gain_grad, output_sum.T, gains[:, 1],
            dense_sum[:, :hidden_n], dense_sum[:, hidden_n:2 * hidden_n], dense_sum[:, 2 * hidden_n:3 * hidden_n].T)


def solution(mesh):
    placed = (
        P(None, None, ("seq", "fsdp"), None),
        P(None, "fsdp", "seq", None),
        P(),
        P(),
        P(("seq", "fsdp")),
        P(("seq", "fsdp"), None),
        P(("seq", "fsdp"), None),
        P(("seq", "fsdp"), None),
        P(("seq", "fsdp"), None),
        P(("seq", "fsdp"), None),
        P(("seq", "fsdp"), None),
        P(None, ("seq", "fsdp")),
        P(None, ("seq", "fsdp")),
        P(None, ("seq", "fsdp")),
        P(),
        P(),
        P(),
        P(None, ("seq", "fsdp")),
        P(("seq", "fsdp")),
        P(("seq", "fsdp"), None),
        P(("seq", "fsdp"), None),
        P(None, ("seq", "fsdp")),
    )
    return jax.shard_map(
        body,
        mesh=mesh,
        in_specs=placed,
        out_specs=(
            P(None, "fsdp", "seq", None),
            P(None, None, ("seq", "fsdp"), None),
            P(("seq", "fsdp")),
            P(("seq", "fsdp"), None),
            P(("seq", "fsdp"), None),
            P(("seq", "fsdp"), None),
            P(("seq", "fsdp"), None),
            P(("seq", "fsdp"), None),
            P(("seq", "fsdp"), None),
            P(None, ("seq", "fsdp")),
            P(None, ("seq", "fsdp")),
            P(None, ("seq", "fsdp")),
            P(),
            P(),
            P(),
            P(None, ("seq", "fsdp")),
            P(("seq", "fsdp")),
            P(("seq", "fsdp"), None),
            P(("seq", "fsdp"), None),
            P(None, ("seq", "fsdp")),
        ),
        check_vma=False,
    )
```

```python
import functools
import jax
import jax.numpy as jnp
from jax import lax
from jax.experimental import pallas as pl
from jax.experimental.pallas import tpu as pltpu
from jax.sharding import PartitionSpec as P

EPS = 1e-6
C = 128
KD = 128
VD = 256
F32 = jnp.float32
BF = jnp.bfloat16
HIGHEST = lax.Precision.HIGHEST

def iota(shape, dim):
    return lax.broadcasted_iota(jnp.int32, shape, dim)

def mm(a, b, ca=1, cb=0):
    return lax.dot_general(a.astype(BF), b.astype(BF), (((ca,), (cb,)), ((), ())), preferred_element_type=F32)

def fine(a, b, ca=1, cb=0):
    a_high, b_high = a.astype(BF), b.astype(BF)
    a_low, b_low = a - a_high.astype(F32), b - b_high.astype(F32)
    return mm(a_high, b_high, ca, cb) + (mm(a_high, b_low, ca, cb) + mm(a_low, b_high, ca, cb))


def exact(a, b):
    return lax.dot_general(a, b, (((1,), (0,)), ((), ())), precision=HIGHEST, preferred_element_type=F32)

def unit_inverses(lows):
    rows, cols = iota((C, C), 0), iota((C, C), 1)
    near = rows // 16 == cols // 16
    packed = [jnp.sum(jnp.where(near, low, 0.0).reshape(C // 16, 16, C), axis=0) for low in lows]
    prow, pcol = iota((16, C), 0), iota((16, C), 1)
    base = (pcol // 16) * 16
    invs = [jnp.where(prow == pcol % 16, 1.0, 0.0).astype(F32) for _ in lows]
    for j in range(15):
        columns = [jnp.take_along_axis(p, base + j, axis=1) for p in packed]
        invs = [inv - column * inv[j:j + 1, :] for inv, column in zip(invs, columns)]
    fulls = [jnp.where(near, jnp.broadcast_to(inv[None], (C // 16, 16, C)).reshape(C, C), 0.0) for inv in invs]
    size = 16
    while size < C:
        below = (rows // (2 * size) == cols // (2 * size)) & (rows // size == cols // size + 1)
        offs = [jnp.where(below, low, 0.0) for low in lows]
        lefts = [mm(full, off) for full, off in zip(fulls, offs)]
        fulls = [full - mm(left, full) for full, left in zip(fulls, lefts)]
        size *= 2
    return fulls


def gates(pre, dlog, dbias):
    arg = pre + dbias
    soft = jnp.maximum(arg, 0.0) + jnp.log1p(jnp.exp(-jnp.abs(arg)))
    log_decay = -jnp.exp(dlog) * soft
    rows, cols = iota((C, C), 0), iota((C, C), 1)
    tri = jnp.where(rows >= cols, 1.0, 0.0).astype(F32)
    cum = exact(tri, log_decay)
    return log_decay, cum

def sig(x):
    return 1.0 / (1.0 + jnp.exp(-x))

def conv_taps(ext_ref, taps, width):
    acc = ext_ref[pl.ds(5, C), :] * taps[0:1, :]
    for i in range(1, 4):
        acc = acc + ext_ref[pl.ds(5 + i, C), :] * taps[i:i + 1, :]
    return acc

def load_ext(qkv, halo, ext_ref, first):
    ahead = halo[8:16, :].astype(F32)
    ext_ref[pl.ds(0, 8), :] = jnp.where(first, 0.0, ahead)
    ext_ref[pl.ds(8, C), :] = qkv.astype(F32)

def forward_kernel(heads, micro, qkv_ref, halo_ref, og_ref, db_ref, taps_ref, small_ref, gain_ref,
                   gated_ref, mix_ref, inv_ref, upd_ref, state_ref, mem_ref, ext_ref):
    step = pl.program_id(0)
    first = step == 0

    @pl.when(first)
    def _():
        mem_ref[...] = jnp.zeros_like(mem_ref)

    taps = taps_ref[...]
    rows, cols = iota((C, C), 0), iota((C, C), 1)
    lower = rows >= cols
    gain = gain_ref[0:1, :]
    units = [(m, h, m * heads + h) for m in range(micro) for h in range(heads)]
    acts, cums, cums_t, rates = [], [], [], []
    for m in range(micro):
        ext = ext_ref.at[m]
        load_ext(qkv_ref[m], halo_ref[m], ext, first)
        act = conv_taps(ext, taps, None)
        acts.append(act * sig(act))
        pre = db_ref[m].astype(F32)
        cums.append(gates(pre, small_ref[0:1, :], small_ref[1:2, :])[1])
        rates.append(sig(pre))
        cums_t.append(jnp.transpose(cums[-1]))
    qs, ks, betas, decays = [], [], [], []
    for m, h, u in units:
        q = acts[m][:, h * KD:(h + 1) * KD]
        k = acts[m][:, (heads + h) * KD:(heads + h + 1) * KD]
        qs.append(q * (lax.rsqrt(jnp.sum(q * q, -1, keepdims=True) + EPS) * KD ** -0.5))
        ks.append(k * lax.rsqrt(jnp.sum(k * k, -1, keepdims=True) + EPS))
        betas.append(rates[m][:, heads + h:heads + h + 1])
        decays.append(jnp.where(lower, jnp.exp(jnp.where(lower, cums[m][:, h:h + 1] - cums_t[m][h:h + 1, :], 0.0)), 0.0))
    dots = [fine(jnp.concatenate([k, q], 0), k, 1, 1) for q, k in zip(qs, ks)]
    lows = [jnp.where(rows > cols, beta * decay * dot[:C], 0.0) for beta, decay, dot in zip(betas, decays, dots)]
    scores = [decay * dot[C:] for decay, dot in zip(decays, dots)]
    invs = unit_inverses(lows)
    growths = [jnp.exp(cums[m][:, h:h + 1]) for m, h, u in units]
    mems = [mem_ref[u] for m, h, u in units]
    from_mems = [mm(jnp.concatenate([growth * k, growth * q], 0), mem) for growth, q, k, mem in zip(growths, qs, ks, mems)]
    rights = [betas[u] * (acts[m][:, 2 * heads * KD + h * VD:2 * heads * KD + (h + 1) * VD] - from_mems[u][:C]) for m, h, u in units]
    upds = [fine(inv, right) for inv, right in zip(invs, rights)]
    for m, h, u in units:
        glast = cums[m][C - 1:C, h:h + 1]
        mem_ref[u] = jnp.exp(glast) * mems[u] + mm(ks[u] * jnp.exp(glast - cums[m][:, h:h + 1]), upds[u], 0, 0)
    outs = [from_mem[C:] + fine(score, upd) for from_mem, score, upd in zip(from_mems, scores, upds)]
    for m, h, u in units:
        state_ref[0, u] = mems[u].astype(state_ref.dtype)
        inv_ref[0, u] = invs[u].astype(inv_ref.dtype)
        upd_ref[0, u] = upds[u].astype(upd_ref.dtype)
        mix = outs[u].astype(BF)
        mix_ref[0, u] = mix
        mix = mix.astype(F32)
        og = og_ref[m, :, h * VD:(h + 1) * VD].astype(F32)
        scale = lax.rsqrt(jnp.mean(mix * mix, -1, keepdims=True) + EPS)
        gated = mix * scale * gain * (og * sig(og))
        gated_ref[0, m, :, h * VD:(h + 1) * VD] = gated.astype(BF)


def mixer_forward(pre, taps, small, gain, heads, shards):
    micro, length, _ = pre.shape
    count = length // C
    units = micro * heads
    qkv_cols, v_cols = heads * (2 * KD + VD), heads * VD
    per = count // shards
    lead = (2 * heads * KD + 2 * v_cols) // 128
    return pl.pallas_call(
        functools.partial(forward_kernel, heads, micro),
        grid=(count,),
        in_specs=[
            pl.BlockSpec((micro, C, qkv_cols), lambda c: (0, c, 0)),
            pl.BlockSpec((micro, 16, qkv_cols), lambda c: (0, jnp.maximum(c * (C // 16) - 1, 0), 0)),
            pl.BlockSpec((micro, C, v_cols), lambda c: (0, c, 2)),
            pl.BlockSpec((micro, C, 128), lambda c: (0, c, lead + 0)),
            pl.BlockSpec((8, qkv_cols), lambda c: (0, 0)),
            pl.BlockSpec((8, 128), lambda c: (0, 0)),
            pl.BlockSpec((8, VD), lambda c: (0, 0)),
        ],
        out_specs=[
            pl.BlockSpec((1, micro, C, v_cols), lambda c: (c // per, 0, c % per, 0)),
            pl.BlockSpec((1, units, C, VD), lambda c: (c, 0, 0, 0)),
            pl.BlockSpec((1, units, C, C), lambda c: (c, 0, 0, 0)),
            pl.BlockSpec((1, units, C, VD), lambda c: (c, 0, 0, 0)),
            pl.BlockSpec((1, units, KD, VD), lambda c: (c, 0, 0, 0)),
        ],
        out_shape=[
            jax.ShapeDtypeStruct((shards, micro, length // shards, v_cols), BF),
            jax.ShapeDtypeStruct((count, units, C, VD), BF),
            jax.ShapeDtypeStruct((count, units, C, C), BF),
            jax.ShapeDtypeStruct((count, units, C, VD), BF),
            jax.ShapeDtypeStruct((count, units, KD, VD), BF),
        ],
        scratch_shapes=[
            pltpu.VMEM((units, KD, VD), F32),
            pltpu.VMEM((micro, C + 8, qkv_cols), F32),
        ],
        compiler_params=pltpu.CompilerParams(
            dimension_semantics=("arbitrary",), vmem_limit_bytes=50 * 1024 * 1024
        ),
        cost_estimate=pl.CostEstimate(flops=units * count * 900_000_000, bytes_accessed=40_000_000, transcendentals=0),
    )(pre, pre, pre, pre, taps, small, gain)


def backward_kernel(heads, micro, qkv_ref, halo_ref, og_ref, db_ref, dgated_ref, mix_ref, inv_ref, upd_ref, state_ref,
                    taps_ref, small_ref, gain_ref,
                    dpre_ref, dtaps_ref, dsmall_ref, dgain_ref, dmem_ref, ext_ref, dy_ref):
    step = pl.program_id(0)
    count = pl.num_programs(0)

    @pl.when(step == 0)
    def _():
        dmem_ref[...] = jnp.zeros_like(dmem_ref)
        dtaps_ref[...] = jnp.zeros_like(dtaps_ref)
        dsmall_ref[...] = jnp.zeros_like(dsmall_ref)
        dgain_ref[...] = jnp.zeros_like(dgain_ref)

    taps = taps_ref[...]
    rows, cols = iota((C, C), 0), iota((C, C), 1)
    lower = rows >= cols
    upper = jnp.where(rows <= cols, 1.0, 0.0).astype(F32)
    gain = gain_ref[0:1, :]
    qk_cols = heads * KD
    strict = rows > cols
    units = [(m, h, m * heads + h) for m in range(micro) for h in range(heads)]
    acts, dgates, pres, logs, cums, cums_t, rates = [], [], [], [], [], [], []
    for m in range(micro):
        ext, dy = ext_ref.at[m], dy_ref.at[m]
        load_ext(qkv_ref[m], halo_ref[m], ext, step == count - 1)
        dy[pl.ds(C, 8), :] = jnp.where(step == 0, 0.0, dy[pl.ds(0, 8), :])
        conv = conv_taps(ext, taps, None)
        gate = sig(conv)
        acts.append(conv * gate)
        dgates.append(gate * (1.0 + conv * (1.0 - gate)))
        pre = db_ref[m].astype(F32)
        log_decay, cum = gates(pre, small_ref[0:1, :], small_ref[1:2, :])
        pres.append(pre)
        logs.append(log_decay)
        cums.append(cum)
        cums_t.append(jnp.transpose(cum))
        rates.append(sig(pre))
    douts = []
    for m, h, u in units:
        mix = mix_ref[0, u].astype(F32)
        og = og_ref[m, :, h * VD:(h + 1) * VD].astype(F32)
        dgated = dgated_ref[0, m, :, h * VD:(h + 1) * VD].astype(F32)
        scale = lax.rsqrt(jnp.mean(mix * mix, -1, keepdims=True) + EPS)
        mixn = mix * scale
        osig = sig(og)
        dog = dgated * mixn * gain * (osig * (1.0 + og * (1.0 - osig)))
        dn = dgated * (og * osig)
        dgain_ref[0:1, :] += jnp.sum(dn * mixn, 0, keepdims=True)
        dn = dn * gain
        douts.append((scale * (dn - mixn * jnp.mean(dn * mixn, -1, keepdims=True))).astype(BF))
        at = 2 * qk_cols + heads * VD + h * VD
        dpre_ref[m, :, at:at + VD] = dog.astype(BF)
    qns, qrs, ks, krs, betas, gcols, decays = [], [], [], [], [], [], []
    for m, h, u in units:
        q0 = acts[m][:, h * KD:(h + 1) * KD]
        k0 = acts[m][:, qk_cols + h * KD:qk_cols + (h + 1) * KD]
        qrs.append(lax.rsqrt(jnp.sum(q0 * q0, -1, keepdims=True) + EPS))
        krs.append(lax.rsqrt(jnp.sum(k0 * k0, -1, keepdims=True) + EPS))
        qns.append(q0 * qrs[u])
        ks.append(k0 * krs[u])
        betas.append(rates[m][:, heads + h:heads + h + 1])
        gcols.append(cums[m][:, h:h + 1])
        decays.append(jnp.where(lower, jnp.exp(jnp.where(lower, gcols[u] - cums_t[m][h:h + 1, :], 0.0)), 0.0))
    root = KD ** -0.5
    dots = [fine(jnp.concatenate([k, qn * root], 0), k, 1, 1) for qn, k in zip(qns, ks)]
    nears = [jnp.where(strict, decay * dot[:C], 0.0) for decay, dot in zip(decays, dots)]
    scores = [decay * dot[C:] for decay, dot in zip(decays, dots)]
    growths = [jnp.exp(gcol) for gcol in gcols]
    glasts = [gcol[C - 1:C, :] for gcol in gcols]
    tails = [jnp.exp(glast - gcol) for glast, gcol in zip(glasts, gcols)]
    ktails = [k * tail for k, tail in zip(ks, tails)]
    dmems = [dmem_ref[u] for m, h, u in units]
    lows = [dmem.astype(BF) for dmem in dmems]
    boths = [jnp.concatenate([upd_ref[0, u], state_ref[0, u]], 0) for m, h, u in units]
    dupds = [mm(score, dout, 0, 0) + mm(ktail, low) for score, dout, ktail, low in zip(scores, douts, ktails, lows)]
    dress = [mm(inv_ref[0, u], dupds[u], 0, 0) for m, h, u in units]
    kins = [growth * k for growth, k in zip(growths, ks)]
    qins = [growth * (qn * root) for growth, qn in zip(growths, qns)]
    for m, h, u in units:
        dmem_ref[u] = jnp.exp(glasts[u]) * dmems[u] + mm(qins[u], douts[u], 0, 0) - mm(betas[u] * kins[u], dress[u], 0, 0)
    ones = [mm(dout, both, 1, 1) for dout, both in zip(douts, boths)]
    twos = [mm(dres, both, 1, 1) for dres, both in zip(dress, boths)]
    dk_tails = [mm(upd_ref[0, u], lows[u], 1, 1) for m, h, u in units]
    dcums = [jnp.zeros((C, 128), F32) for m in range(micro)]
    drates = [jnp.zeros((C, 128), F32) for m in range(micro)]
    lane = iota((C, 128), 1)
    last = iota((C, 1), 0) == C - 1
    dqks, dkks = [], []
    for m, h, u in units:
        dscores = jnp.where(lower, ones[u][:, :C], 0.0)
        dlow = jnp.where(strict, -twos[u][:, :C], 0.0)
        pull_low = dlow * nears[u]
        pulls = dscores * scores[u] + betas[u] * pull_low
        dk_kin = twos[u][:, C:] * kins[u]
        dk_ktail = dk_tails[u] * ktails[u]
        in_parts = jnp.sum(ones[u][:, C:] * qins[u] - betas[u] * dk_kin - dk_ktail + pulls, -1, keepdims=True)
        tail_sum = jnp.sum(jnp.sum(dk_ktail, -1, keepdims=True), 0, keepdims=True)
        mem_sum = jnp.sum(jnp.sum(dmems[u] * state_ref[0, u].astype(F32), -1, keepdims=True), 0, keepdims=True)
        across = jnp.transpose(jnp.broadcast_to(jnp.sum(pulls, 0, keepdims=True), (C, C)))[:, 0:1]
        dcum_col = in_parts - across + jnp.where(last, tail_sum + jnp.exp(glasts[u]) * mem_sum, 0.0)
        v = acts[m][:, 2 * qk_cols + h * VD:2 * qk_cols + (h + 1) * VD]
        dbeta = jnp.sum(dress[u] * v, -1, keepdims=True) + jnp.sum(pull_low - dk_kin, -1, keepdims=True)
        dcums[m] = jnp.where(lane == h, dcum_col, dcums[m])
        drates[m] = jnp.where(lane == heads + h, dbeta, drates[m])
        dqks.append(dscores * decays[u])
        dkks.append(dlow * decays[u] * betas[u])
    lefts = [mm(jnp.concatenate([dqk, dkk], 0), k) for dqk, dkk, k in zip(dqks, dkks, ks)]
    rights = [mm(dqk, qn * root, 0, 0) + mm(dkk, k, 0, 0) for dqk, dkk, qn, k in zip(dqks, dkks, qns, ks)]
    for m, h, u in units:
        dy, dgate = dy_ref.at[m], dgates[m]
        dq = (lefts[u][:C] + growths[u] * ones[u][:, C:]) * root
        dk = lefts[u][C:] + rights[u] - (growths[u] * betas[u]) * twos[u][:, C:] + tails[u] * dk_tails[u]
        dq = qrs[u] * (dq - qns[u] * jnp.sum(dq * qns[u], -1, keepdims=True))
        dk = krs[u] * (dk - ks[u] * jnp.sum(dk * ks[u], -1, keepdims=True))
        for part, at, wide in ((dq, h * KD, KD), (dk, qk_cols + h * KD, KD), (betas[u] * dress[u], 2 * qk_cols + h * VD, VD)):
            dy[pl.ds(0, C), at:at + wide] = part * dgate[:, at:at + wide]
    speed = -jnp.exp(small_ref[0:1, :])
    for m in range(micro):
        ext, dy = ext_ref.at[m], dy_ref.at[m]
        grad = dy[pl.ds(0, C), :]
        dx = dy[pl.ds(3, C), :] * taps[0:1, :]
        for i in range(1, 4):
            dx = dx + dy[pl.ds(3 - i, C), :] * taps[i:i + 1, :]
        dpre_ref[m, :, 0:2 * qk_cols + heads * VD] = dx.astype(BF)
        for i in range(4):
            dtaps_ref[i:i + 1, :] += jnp.sum(grad * ext[pl.ds(5 + i, C), :], 0, keepdims=True)
        dlog = exact(upper, dcums[m])
        ddecay = dlog * speed * sig(pres[m] + small_ref[1:2, :])
        dsmall_ref[0:1, :] += jnp.sum(dlog * logs[m], 0, keepdims=True)
        dsmall_ref[1:2, :] += jnp.sum(ddecay, 0, keepdims=True)
        ddb = ddecay + drates[m] * rates[m] * (1.0 - rates[m])
        at = 2 * qk_cols + 2 * heads * VD
        dpre_ref[m, :, at:at + 128] = ddb.astype(BF)


def mixer_backward(pre, dgated, saved, taps, small, gain, heads):
    mix, inv, upd, state = saved
    shards, micro, part, v_cols = dgated.shape
    length, width = pre.shape[1:]
    count = length // C
    units = micro * heads
    qkv_cols = heads * (2 * KD + VD)
    per = count // shards
    lead = (2 * heads * KD + 2 * v_cols) // 128
    end = count - 1
    keep = lambda *s: pl.BlockSpec((1, units) + s, lambda c: (end - c, 0, 0, 0))
    return pl.pallas_call(
        functools.partial(backward_kernel, heads, micro),
        grid=(count,),
        in_specs=[
            pl.BlockSpec((micro, C, qkv_cols), lambda c: (0, end - c, 0)),
            pl.BlockSpec((micro, 16, qkv_cols), lambda c: (0, jnp.maximum((end - c) * (C // 16) - 1, 0), 0)),
            pl.BlockSpec((micro, C, v_cols), lambda c: (0, end - c, 2)),
            pl.BlockSpec((micro, C, 128), lambda c: (0, end - c, lead)),
            pl.BlockSpec((1, micro, C, v_cols), lambda c: ((end - c) // per, 0, (end - c) % per, 0)),
            keep(C, VD), keep(C, C), keep(C, VD), keep(KD, VD),
            pl.BlockSpec((8, qkv_cols), lambda c: (0, 0)),
            pl.BlockSpec((8, 128), lambda c: (0, 0)),
            pl.BlockSpec((8, VD), lambda c: (0, 0)),
        ],
        out_specs=[
            pl.BlockSpec((micro, C, width), lambda c: (0, end - c, 0)),
            pl.BlockSpec((8, qkv_cols), lambda c: (0, 0)),
            pl.BlockSpec((8, 128), lambda c: (0, 0)),
            pl.BlockSpec((8, VD), lambda c: (0, 0)),
        ],
        out_shape=[
            jax.ShapeDtypeStruct((micro, length, width), BF),
            jax.ShapeDtypeStruct((8, qkv_cols), F32),
            jax.ShapeDtypeStruct((8, 128), F32),
            jax.ShapeDtypeStruct((8, VD), F32),
        ],
        scratch_shapes=[
            pltpu.VMEM((units, KD, VD), F32),
            pltpu.VMEM((micro, C + 8, qkv_cols), F32),
            pltpu.VMEM((micro, C + 8, qkv_cols), F32),
        ],
        compiler_params=pltpu.CompilerParams(
            dimension_semantics=("arbitrary",), vmem_limit_bytes=50 * 1024 * 1024
        ),
        cost_estimate=pl.CostEstimate(flops=units * count * 1_600_000_000, bytes_accessed=60_000_000, transcendentals=0),
    )(pre, pre, pre, pre, dgated, mix, inv, upd, state, taps, small, gain)


MESH_ID = pl.DeviceIdType.MESH


def start_kernel(shards, groups, rows_y, micro, tok_ref, pack_ref, every_ref, wm_ref,
                 local_sem, send_sem, one_sem, z_sem, y_sem, deal_sem, swap_sem):
    s, f = lax.axis_index("seq"), lax.axis_index("fsdp")
    deep = groups // rows_y
    z, y = f // rows_y, lax.rem(f, rows_y)
    barrier = pltpu.get_barrier_semaphore()
    for d in range(1, shards):
        pl.semaphore_signal(barrier, inc=1, device_id=(jnp.bitwise_xor(s, d), f), device_id_type=MESH_ID)
    for k in range(1, groups):
        pl.semaphore_signal(barrier, inc=1, device_id=(s, lax.rem(f + k, groups)), device_id_type=MESH_ID)
    pl.semaphore_wait(barrier, shards + groups - 2)

    sent = []

    def send(src, dst, sem, device):
        at = len(sent)
        copy = pltpu.make_async_remote_copy(src, dst, send_sem.at[at], sem, device_id=device, device_id_type=MESH_ID)
        copy.start()
        sent.append(copy)
        return copy

    place = wm_ref.at[s, z, y]
    first = []
    for d in range(1, shards):
        to = jnp.bitwise_xor(s, d)
        first.append(send(pack_ref.at[to], place, one_sem.at[d], (to, f)))
    mine = pltpu.make_async_copy(pack_ref.at[s], place, local_sem.at[0])
    mine.start()
    keeps = []
    for m in range(micro):
        keep = pltpu.make_async_copy(tok_ref.at[m, f], every_ref.at[m, s, f], local_sem.at[1 + m])
        keep.start()
        keeps.append(keep)

    def deal(m):
        return [send(tok_ref.at[m, lax.rem(f + k, groups)], every_ref.at[m, s, f], deal_sem.at[m, k],
                     (s, lax.rem(f + k, groups))) for k in range(1, groups)]

    dealt = [deal(0)]
    columns = []
    mine.wait()
    for d in range(shards):
        block = jnp.bitwise_xor(s, d)
        if d:
            first[d - 1].wait_recv()
        columns.append([send(wm_ref.at[block, z, y], wm_ref.at[block, z, y], z_sem.at[d, k],
                             (s, lax.rem(z + k, deep) * rows_y + y)) for k in range(1, deep)])
    for m in range(1, micro):
        dealt.append(deal(m))

    bits = []
    bit = shards // 2
    while bit:
        bits.append(bit)
        bit //= 2

    def swap(m, level):
        bit = bits[level]
        held = [0]
        for b in bits[:level]:
            held = held + [h | b for h in held]
        return [send(every_ref.at[m, jnp.bitwise_xor(s, h)], every_ref.at[m, jnp.bitwise_xor(s, h)],
                     swap_sem.at[m, level, i], (jnp.bitwise_xor(s, bit), f)) for i, h in enumerate(held)]

    rows_of = []
    swaps = {}
    for m in range(micro):
        keeps[m].wait()
        for copy in dealt[m]:
            copy.wait_recv()
        swaps[m, 0] = swap(m, 0)
        if m == 0:
            for d in range(shards):
                block = jnp.bitwise_xor(s, d)
                for copy in columns[d]:
                    copy.wait_recv()
                rows_of.append([send(wm_ref.at[block, :, y], wm_ref.at[block, :, y], y_sem.at[d, j],
                                     (s, z * rows_y + lax.rem(y + j, rows_y))) for j in range(1, rows_y)])
    for level in range(1, len(bits)):
        for m in range(micro):
            for copy in swaps[m, level - 1]:
                copy.wait_recv()
            swaps[m, level] = swap(m, level)
    for m in range(micro):
        for copy in swaps[m, len(bits) - 1]:
            copy.wait_recv()
    for d in range(shards):
        for copy in rows_of[d]:
            copy.wait_recv()
    for copy in sent:
        copy.wait_send()


def start_exchange(tok, pack, shards, groups):
    micro, _, own, width = tok.shape
    rows_y = max(shards // 2, 1)
    deep = groups // rows_y
    levels = max(shards.bit_length() - 1, 1)
    copies = (shards - 1) + micro * (groups - 1) + shards * (deep - 1) + shards * (rows_y - 1) + micro * (shards - 1)
    hbm = pl.BlockSpec(memory_space=pl.ANY)
    return pl.pallas_call(
        functools.partial(start_kernel, shards, groups, rows_y, micro),
        in_specs=[hbm, hbm],
        out_specs=[hbm, hbm],
        out_shape=[
            jax.ShapeDtypeStruct((micro, shards, groups, own, width), tok.dtype),
            jax.ShapeDtypeStruct((shards, deep, rows_y) + pack.shape[1:], pack.dtype),
        ],
        scratch_shapes=[
            pltpu.SemaphoreType.DMA((1 + micro,)),
            pltpu.SemaphoreType.DMA((copies,)),
            pltpu.SemaphoreType.DMA((shards,)),
            pltpu.SemaphoreType.DMA((shards, deep)),
            pltpu.SemaphoreType.DMA((shards, rows_y)),
            pltpu.SemaphoreType.DMA((micro, groups)),
            pltpu.SemaphoreType.DMA((micro, levels, max(shards // 2, 1))),
        ],
        compiler_params=pltpu.CompilerParams(collective_id=0, has_side_effects=True),
    )(tok, pack)


def finish_kernel(shards, deep, rows_y, dw_ref, wo_ref, little_ref, out_ref, wo_sum_ref, total_ref,
                  y_buf, y_wo, z_buf, z_wo, mid, mid_wo, fin, little_buf, little_mid,
                  send_sem, y_sem, z_sem, s_sem, little_sem):
    s, f = lax.axis_index("seq"), lax.axis_index("fsdp")
    z, y = f // rows_y, lax.rem(f, rows_y)
    y_peers = [(s, z * rows_y + lax.rem(y + j, rows_y)) for j in range(1, rows_y)]
    z_peers = [(s, lax.rem(z + k, deep) * rows_y + y) for k in range(1, deep)]
    s_peers = [(jnp.bitwise_xor(s, d), f) for d in range(1, shards)]
    barrier = pltpu.get_barrier_semaphore()
    for peer in y_peers + z_peers + s_peers:
        pl.semaphore_signal(barrier, inc=1, device_id=peer, device_id_type=MESH_ID)
    pl.semaphore_wait(barrier, len(y_peers + z_peers + s_peers))

    sent = []

    def send(src, dst, sem, device):
        copy = pltpu.make_async_remote_copy(src, dst, send_sem.at[len(sent)], sem, device_id=device, device_id_type=MESH_ID)
        copy.start()
        sent.append(copy)
        return copy

    blocks = [jnp.bitwise_xor(s, d) for d in range(shards)]
    in_y = [[send(dw_ref.at[b, :, lax.rem(y + j, rows_y)], y_buf.at[j - 1, d], y_sem.at[j, d], y_peers[j - 1])
             for j in range(1, rows_y)] for d, b in enumerate(blocks)]
    in_y.append([send(wo_ref.at[:, lax.rem(y + j, rows_y)], y_wo.at[j - 1], y_sem.at[j, shards], y_peers[j - 1])
                 for j in range(1, rows_y)])
    little_copies = [send(little_ref, little_buf.at[j], little_sem.at[j], y_peers[j]) for j in range(rows_y - 1)]
    in_z = []
    for d, b in enumerate(blocks):
        for copy in in_y[d]:
            copy.wait_recv()
        for part in range(deep):
            acc = dw_ref[b, part, y].astype(F32)
            for j in range(rows_y - 1):
                acc = acc + y_buf[j, d, part].astype(F32)
            mid[d, part] = acc.astype(BF)
        in_z.append([send(mid.at[d, lax.rem(z + k, deep)], z_buf.at[k - 1, d], z_sem.at[k, d], z_peers[k - 1])
                     for k in range(1, deep)])
    for copy in in_y[shards]:
        copy.wait_recv()
    for part in range(deep):
        acc = wo_ref[part, y].astype(F32)
        for j in range(rows_y - 1):
            acc = acc + y_wo[j, part].astype(F32)
        mid_wo[part] = acc.astype(BF)
    in_z.append([send(mid_wo.at[lax.rem(z + k, deep)], z_wo.at[k - 1], z_sem.at[k, shards], z_peers[k - 1])
                 for k in range(1, deep)])
    at = rows_y - 1
    for copy in little_copies:
        copy.wait_recv()
    little = little_ref[...]
    for j in range(rows_y - 1):
        little = little + little_buf[j]
    little_mid[0] = little
    little_copies = [send(little_mid.at[0], little_buf.at[at + k], little_sem.at[at + k], z_peers[k]) for k in range(deep - 1)]
    in_s = []
    for d, b in enumerate(blocks):
        for copy in in_z[d]:
            copy.wait_recv()
        acc = mid[d, z].astype(F32)
        for k in range(deep - 1):
            acc = acc + z_buf[k, d].astype(F32)
        if d:
            fin[d - 1] = acc.astype(BF)
            in_s.append(send(fin.at[d - 1], out_ref.at[s], s_sem.at[d], s_peers[d - 1]))
        else:
            out_ref[s] = acc.astype(BF)
    for copy in in_z[shards]:
        copy.wait_recv()
    acc = mid_wo[z].astype(F32)
    for k in range(deep - 1):
        acc = acc + z_wo[k].astype(F32)
    wo_sum_ref[...] = acc
    for copy in little_copies:
        copy.wait_recv()
    for k in range(deep - 1):
        little = little + little_buf[at + k]
    little_mid[1] = little
    at += deep - 1
    little_copies = [send(little_mid.at[1], little_buf.at[at + d], little_sem.at[at + d], s_peers[d]) for d in range(shards - 1)]
    for copy in little_copies:
        copy.wait_recv()
    for d in range(shards - 1):
        little = little + little_buf[at + d]
    total_ref[...] = little
    for copy in in_s:
        copy.wait_recv()
    for copy in sent:
        copy.wait_send()


def finish_sums(dw, wo, little, shards, groups):
    rows_y = max(shards // 2, 1)
    deep = groups // rows_y
    own, cols = dw.shape[2:]
    wide = wo.shape[2]
    small_n = (rows_y - 1) + (deep - 1) + (shards - 1)
    copies = (shards + 2) * (rows_y + deep - 2) + 2 * (shards - 1)
    vmem = pl.BlockSpec(memory_space=pltpu.VMEM)
    return pl.pallas_call(
        functools.partial(finish_kernel, shards, deep, rows_y),
        in_specs=[vmem] * 3,
        out_specs=[vmem] * 3,
        out_shape=[
            jax.ShapeDtypeStruct((shards, own, cols), BF),
            jax.ShapeDtypeStruct((own, wide), F32),
            jax.ShapeDtypeStruct(little.shape, F32),
        ],
        scratch_shapes=[
            pltpu.VMEM((max(rows_y - 1, 1), shards, deep, own, cols), BF),
            pltpu.VMEM((max(rows_y - 1, 1), deep, own, wide), BF),
            pltpu.VMEM((max(deep - 1, 1), shards, own, cols), BF),
            pltpu.VMEM((max(deep - 1, 1), own, wide), BF),
            pltpu.VMEM((shards, deep, own, cols), BF),
            pltpu.VMEM((deep, own, wide), BF),
            pltpu.VMEM((max(shards - 1, 1), own, cols), BF),
            pltpu.VMEM((small_n,) + little.shape, F32),
            pltpu.VMEM((2,) + little.shape, F32),
            pltpu.SemaphoreType.DMA((copies,)),
            pltpu.SemaphoreType.DMA((rows_y, shards + 1)),
            pltpu.SemaphoreType.DMA((deep, shards + 1)),
            pltpu.SemaphoreType.DMA((shards,)),
            pltpu.SemaphoreType.DMA((small_n,)),
        ],
        compiler_params=pltpu.CompilerParams(collective_id=1, has_side_effects=True, vmem_limit_bytes=48 * 1024 * 1024),
    )(dw.reshape(shards, deep, rows_y, own, cols), wo.reshape(deep, rows_y, own, wide), little)


def rms_scale(values, gain):
    return values * lax.rsqrt(jnp.mean(values * values, -1, keepdims=True) + EPS) * gain


def swish_gate(gate_val, upper_val):
    return jax.nn.silu(gate_val) * upper_val


def product(left, right):
    return jnp.dot(left, right, preferred_element_type=F32)


def outer_sum(left, right):
    return lax.dot_general(left, right, (((0,), (0,)), ((), ())), preferred_element_type=F32)


def back_through(left, right):
    return lax.dot_general(left, right, (((1,), (1,)), ((), ())), preferred_element_type=F32)


def take_rows(source, order):
    return jnp.take(source, order, axis=0)


BOTH = ("seq", "fsdp")


def bits_of(size):
    return [1 << i for i in reversed(range(size.bit_length() - 1))]


def reduce_halves(values, names, sizes, order, done=(), last=True):
    left = [(name, bit) for name, size in zip(names, sizes) for bit in bits_of(size) if (name, bit) not in done]
    if not done:
        values = values.reshape((2,) * len(left) + values.shape[len(names):])
    for name, bit in order:
        at = left.index((name, bit))
        side = (lax.axis_index(name) // bit) % 2
        away = lax.dynamic_index_in_dim(values, 1 - side, at, keepdims=False)
        kept = lax.dynamic_index_in_dim(values, side, at, keepdims=False)
        came = lax.ppermute(away, name, [(i, i ^ bit) for i in range(sizes[names.index(name)])])
        values = kept.astype(F32) + came.astype(F32)
        left.pop(at)
        if left or not last:
            values = values.astype(BF)
    return values


def body(tokens, cotangent, seq_lengths, seq_slots, norm_gain, w_query, w_key, w_value, w_decay, w_beta, w_outgate,
         query_filter, key_filter, value_filter, decay_log, decay_bias, head_gain, w_output, ffn_gain, w_gate, w_up, w_down):
    shards, groups = lax.axis_size("seq"), lax.axis_size("fsdp")
    group_pos, shard_pos = lax.axis_index("fsdp"), lax.axis_index("seq")
    micro, slots = seq_slots.shape
    width = tokens.shape[3]
    part = cotangent.shape[2]
    length = part * shards
    own = w_query.shape[0]
    heads = decay_log.shape[0] // shards
    taps_n = query_filter.shape[0]
    lanes = 128

    def by_head(weight):
        return weight.reshape(own, shards, weight.shape[1] // shards)

    def spread(columns):
        return jnp.broadcast_to(columns[:, None, :], (own, shards, columns.shape[1]))

    def filter_columns(taps):
        times = taps.shape[1] // own
        return taps.reshape(taps_n, times, own).transpose(2, 1, 0).reshape(own, times * taps_n)

    filters = jnp.concatenate([filter_columns(query_filter), filter_columns(key_filter), filter_columns(value_filter)], 1)
    extra = jnp.concatenate([norm_gain[:, None], ffn_gain[:, None], filters], 1)
    spare = lanes - 2 * heads - extra.shape[1]
    packed = jnp.concatenate(
        [by_head(w_query), by_head(w_key), by_head(w_value), by_head(w_outgate), by_head(w_decay), by_head(w_beta),
         spread(extra), jnp.zeros((own, shards, spare), BF)], 2).transpose(1, 0, 2)

    slot_ids = jnp.arange(slots, dtype=jnp.int32)
    matches = seq_slots[:, :, None] == slot_ids[None, None, :]
    source_of = jnp.sum(jnp.where(matches, slot_ids[None, :, None], 0), axis=1)
    slot_length = jnp.sum(jnp.where(matches, seq_lengths[:, :, None], 0), axis=1)
    units = micro
    local_length = lax.dynamic_slice_in_dim(slot_length, group_pos, 1, 1).reshape(units)
    row_ids = shard_pos * part + jnp.arange(part, dtype=jnp.int32)
    valid = (row_ids[None, :] < local_length[:, None]).astype(F32)[..., None]
    ordered = jax.vmap(take_rows)(tokens, source_of)
    everything, w_mixer = start_exchange(ordered, packed, shards, groups)
    everything = everything.reshape(units, length, width)
    w_mixer = w_mixer.reshape(width, packed.shape[2])
    rows = units * part
    inputs = lax.dynamic_slice_in_dim(everything, shard_pos * part, part, 1).reshape(rows, width)
    side = w_mixer[:, w_mixer.shape[1] - lanes:].astype(F32)
    at = 2 * heads
    norm_row, ffn_row = side[:, at], side[:, at + 1]
    rows_of = width // shards
    mine = lax.dynamic_slice_in_dim(side, shard_pos * rows_of, rows_of, 0)[:, at + 2:at + 2 + filters.shape[1]]

    def filter_rows(cols):
        times = cols.shape[1] // taps_n
        return cols.reshape(groups, own, times, taps_n).transpose(3, 0, 2, 1).reshape(taps_n, groups * times * own)

    taps = jnp.concatenate([filter_rows(mine[:, :taps_n]), filter_rows(mine[:, taps_n:2 * taps_n]), filter_rows(mine[:, 2 * taps_n:])], 1)
    taps = jnp.pad(taps, ((0, 8 - taps_n), (0, 0)))
    small = jnp.stack([lax.dynamic_slice_in_dim(decay_log, shard_pos * heads, heads, 0),
                       lax.dynamic_slice_in_dim(decay_bias, shard_pos * heads, heads, 0)])
    small = jnp.pad(small, ((0, 6), (0, lanes - heads)))
    gain = jnp.broadcast_to(head_gain.astype(F32)[None], (8, head_gain.shape[0]))
    dense = jnp.concatenate([w_output.T, w_gate, w_up, w_down.T], 1)
    dense, everything = lax.optimization_barrier((dense, everything))
    w_dense = lax.all_gather(dense, BOTH, axis=0, tiled=True)
    hidden_n, mixer_n = w_gate.shape[1], w_output.shape[0]
    w_out_t = w_dense[:, :mixer_n]
    w_gate_all, w_up_all = w_dense[:, mixer_n:mixer_n + hidden_n], w_dense[:, mixer_n + hidden_n:mixer_n + 2 * hidden_n]
    w_down_t = w_dense[:, mixer_n + 2 * hidden_n:]

    normed = rms_scale(everything.astype(F32), norm_row).astype(BF).reshape(units * length, width)
    pre = product(normed, w_mixer).astype(BF).reshape(units, length, w_mixer.shape[1])
    gated, *saved = mixer_forward(pre, taps, small, gain, heads, shards)
    gated = lax.all_to_all(gated, "seq", split_axis=0, concat_axis=0, tiled=True)
    v_cols = gated.shape[-1]
    gated = gated.reshape(shards, rows, v_cols).transpose(1, 0, 2).reshape(rows, shards * v_cols)

    residual = inputs.astype(F32)
    attended = residual + back_through(gated, w_out_t)
    ffn_in, ffn_back = jax.vjp(rms_scale, attended, ffn_row)
    ffn_in = ffn_in.astype(BF)
    hidden, hidden_back = jax.vjp(swish_gate, product(ffn_in, w_gate_all), product(ffn_in, w_up_all))
    hidden = hidden.astype(BF)
    output = attended + back_through(hidden, w_down_t)
    mixed = (output.reshape(units, part, width) * valid).reshape(micro, 1, part, width)
    cot = (cotangent.reshape(units, part, width).astype(F32) * valid).reshape(rows, width)
    down_in = cot.astype(BF)
    down_grad = outer_sum(down_in, hidden).astype(BF)
    gate_back, upper_back = hidden_back(product(down_in, w_down_t))
    gate_back, upper_back = gate_back.astype(BF), upper_back.astype(BF)
    gate_grad = outer_sum(ffn_in, gate_back).astype(BF)
    up_grad = outer_sum(ffn_in, upper_back).astype(BF)
    attended_back, ffn_gain_grad = ffn_back(back_through(gate_back, w_gate_all) + back_through(upper_back, w_up_all))
    attended_back = cot + attended_back
    branch_in = attended_back.astype(BF)
    output_grad = outer_sum(branch_in, gated).astype(BF)
    dense_grad = jnp.concatenate([gate_grad, up_grad, down_grad], 1)
    gated_back = product(branch_in, w_out_t).astype(BF)
    gated_back = gated_back.reshape(rows, shards, v_cols).transpose(1, 0, 2).reshape(shards, units, part, v_cols)
    gated_back = lax.all_to_all(gated_back, "seq", split_axis=0, concat_axis=0, tiled=True)

    seq_order = [("seq", bit) for bit in reversed(bits_of(shards))]
    group_order = [("fsdp", bit) for bit in reversed(bits_of(groups))]
    order = seq_order + group_order
    output_grad = output_grad.reshape(shards, groups, own, output_grad.shape[1])
    output_sum = reduce_halves(output_grad, BOTH, (shards, groups), order[:1], last=False)
    gated_back, dense_grad, output_sum = lax.optimization_barrier((gated_back, dense_grad, output_sum))
    dense_sum = lax.psum_scatter(dense_grad, BOTH, scatter_dimension=0, tiled=True)
    output_sum = reduce_halves(output_sum, BOTH, (shards, groups), seq_order[1:], done=order[:1], last=False)

    dpre, dtaps, dsmall, dgain = mixer_backward(pre, gated_back, saved, taps, small, gain, heads)
    dpre, output_sum = lax.optimization_barrier((dpre, output_sum))
    normed_back = []
    for m in range(units):
        partial = back_through(dpre[m], w_mixer).astype(BF).reshape(shards, part, width)
        normed_back.append(reduce_halves(partial, ("seq",), (shards,), seq_order))
    dpre = dpre.reshape(units * length, dpre.shape[2])
    dw = outer_sum(normed, dpre).astype(BF)
    main = dw.shape[1] - lanes
    used = main + at
    norm_gain_part = jnp.sum(dw[:, :used].astype(F32) * w_mixer[:, :used].astype(F32), 1) / norm_row

    def grad_columns(grads):
        times = grads.shape[1] // rows_of
        return grads.reshape(taps_n, groups, times, own).transpose(1, 3, 2, 0).reshape(rows_of, times * taps_n)

    qk_cols = heads * KD
    filter_part = jnp.concatenate([grad_columns(dtaps[:taps_n, :qk_cols]), grad_columns(dtaps[:taps_n, qk_cols:2 * qk_cols]), grad_columns(dtaps[:taps_n, 2 * qk_cols:])], 1)
    filter_part = lax.dynamic_update_slice_in_dim(jnp.zeros((width, filter_part.shape[1]), F32), filter_part, shard_pos * rows_of, 0)
    side = jnp.concatenate([norm_gain_part[:, None], ffn_gain_grad[:, None], filter_part], 1).astype(BF)
    dw = lax.dynamic_update_slice(dw, side, (0, used)).reshape(shards, groups, own, dw.shape[1])

    def placed(values):
        return lax.dynamic_update_slice_in_dim(jnp.zeros((lanes,), F32), values, shard_pos * heads, 0)

    little = jnp.concatenate([placed(dsmall[0, :heads])[None], placed(dsmall[1, :heads])[None], dgain[0].reshape(-1, lanes)])
    little = jnp.pad(little, ((0, 8 - little.shape[0]), (0, 0)))
    dw, output_sum, little = finish_sums(dw, output_sum.reshape(groups, own, output_sum.shape[-1]), little, shards, groups)
    dw = dw.astype(F32)
    count = decay_log.shape[0]
    decay_log_grad, decay_bias_grad, head_gain_grad = little[0, :count], little[1, :count], little[2:2 + dgain.shape[1] // lanes].reshape(-1)

    def columns(start, stop):
        return dw[:, :, start:stop].transpose(1, 0, 2).reshape(own, shards * (stop - start))

    hv = heads * VD
    query_grad, key_grad = columns(0, qk_cols), columns(qk_cols, 2 * qk_cols)
    value_grad, outgate_grad = columns(2 * qk_cols, 2 * qk_cols + hv), columns(2 * qk_cols + hv, main)
    decay_grad, beta_grad = columns(main, main + heads), columns(main + heads, main + 2 * heads)
    gains = jnp.sum(dw[:, :, main + at:main + at + 2], 0)
    filter_own = lax.dynamic_index_in_dim(dw, shard_pos, 0, keepdims=False)[:, main + at + 2:main + at + 2 + filters.shape[1]]

    def filter_grad(cols):
        times = cols.shape[1] // taps_n
        return cols.reshape(own, times, taps_n).transpose(2, 1, 0).reshape(taps_n, times * own)

    filter_grads = (filter_grad(filter_own[:, :taps_n]), filter_grad(filter_own[:, taps_n:2 * taps_n]), filter_grad(filter_own[:, 2 * taps_n:]))

    home = []
    for m in range(units):
        _, norm_back = jax.vjp(rms_scale, residual[m * part:(m + 1) * part], norm_row)
        input_back, _ = norm_back(normed_back[m])
        slot_grad = (attended_back[m * part:(m + 1) * part] + input_back).astype(BF).reshape(groups, own, width)
        back = lax.all_to_all(slot_grad, "fsdp", split_axis=0, concat_axis=0, tiled=True)
        home.append(take_rows(back, seq_slots[m]))
    tokens_grad = jnp.stack(home).astype(F32)
    dense_sum = dense_sum.astype(F32)
    return (mixed, tokens_grad, gains[:, 0], query_grad, key_grad, value_grad, decay_grad, beta_grad, outgate_grad,
            *filter_grads, decay_log_grad, decay_bias_grad, head_gain_grad, output_sum.T, gains[:, 1],
            dense_sum[:, :hidden_n], dense_sum[:, hidden_n:2 * hidden_n], dense_sum[:, 2 * hidden_n:3 * hidden_n].T)


def solution(mesh):
    placed = (
        P(None, None, ("seq", "fsdp"), None),
        P(None, "fsdp", "seq", None),
        P(),
        P(),
        P(("seq", "fsdp")),
        P(("seq", "fsdp"), None),
        P(("seq", "fsdp"), None),
        P(("seq", "fsdp"), None),
        P(("seq", "fsdp"), None),
        P(("seq", "fsdp"), None),
        P(("seq", "fsdp"), None),
        P(None, ("seq", "fsdp")),
        P(None, ("seq", "fsdp")),
        P(None, ("seq", "fsdp")),
        P(),
        P(),
        P(),
        P(None, ("seq", "fsdp")),
        P(("seq", "fsdp")),
        P(("seq", "fsdp"), None),
        P(("seq", "fsdp"), None),
        P(None, ("seq", "fsdp")),
    )
    return jax.shard_map(
        body,
        mesh=mesh,
        in_specs=placed,
        out_specs=(
            P(None, "fsdp", "seq", None),
            P(None, None, ("seq", "fsdp"), None),
            P(("seq", "fsdp")),
            P(("seq", "fsdp"), None),
            P(("seq", "fsdp"), None),
            P(("seq", "fsdp"), None),
            P(("seq", "fsdp"), None),
            P(("seq", "fsdp"), None),
            P(("seq", "fsdp"), None),
            P(None, ("seq", "fsdp")),
            P(None, ("seq", "fsdp")),
            P(None, ("seq", "fsdp")),
            P(),
            P(),
            P(),
            P(None, ("seq", "fsdp")),
            P(("seq", "fsdp")),
            P(("seq", "fsdp"), None),
            P(("seq", "fsdp"), None),
            P(None, ("seq", "fsdp")),
        ),
        check_vma=False,
    )
```
